512 devices in a mesh: slab: 8 (over y), orb: 64 (over x, z, core).
Axes of the slice: x: 4, y: 8, z: 8, core: 2. Of those that a mesh axis runs over, the one named last changes fastest.
Arguments:
- orbitals_t: bfloat16 [2048, 65536], P('orb', 'slab'), may hold values from -6 to 6
- tiles: bfloat16 [896, 128, 128], P('slab'), may hold values from -0.375 to 0.375
- tile_rows: int32 [896], P('slab'), may hold values from 0 to 63
- tile_cols: int32 [896], P('slab'), may hold values from -2 to 65, as said below
- row_counts: int32 [512], P('slab'), may hold values from 1 to 128, 49152 in all
- bounds: float32 [3], replicated, may hold values from 0 to 1
- rotation: bfloat16 [2048, 2048], P('orb'), may hold values from -0.125 to 0.125
Outputs:
- rotated_t: bfloat16 [2048, 65536], P('orb', 'slab')
The draws below stay inside these ranges and needn't reach their ends.
Inputs may be any that keep to these rules, and one draw needn't show every extreme that they name: `tile_cols`: within every slab, the first 64 tiles are the diagonal tiles of row blocks 0 to 63 in order; a tile's column block lies within 2 blocks of its row block; in every slab some tile of row block 0 has column block -2 and some tile of row block 63 has column block 65.
All inputs are finite; a program needn't handle non-finite values. No bound on the sum of `row_counts` on one device may be relied on, other than what follows from the above.
Results may differ from the reference program's by a relative error of at most 0.006.
Values may be sent and summed in bfloat16 or wider, within the bound.
A program may use at most 64 MiB of HBM per device.

```python
import math
import jax
import jax.numpy as jnp
import numpy as np
from jax import lax

NORB = 2048
TILE = 128
HB = 2
BLK_SLAB = 64
TILES_SLAB = 112
NBLK = 512
ROWS = 65536
N_SLAB = 8


def tile_layout(key):
    key_one, key_two, key_three, key_four = jax.random.split(jax.random.fold_in(key, 7), 4)
    extra = TILES_SLAB - BLK_SLAB
    extra_rows = jax.random.randint(key_one, (N_SLAB, extra), 0, BLK_SLAB)
    magnitude = jax.random.randint(key_two, (N_SLAB, extra), 1, HB + 1)
    signs = jax.random.randint(key_three, (N_SLAB, extra), 0, 2) * 2 - 1
    offsets = magnitude * signs
    extra_rows = extra_rows.at[:, 0].set(0).at[:, 1].set(BLK_SLAB - 1)
    offsets = offsets.at[:, 0].set(-HB).at[:, 1].set(HB)
    extra_cols = extra_rows + offsets
    slab_keys = jax.random.split(key_four, N_SLAB)
    orders = jax.vmap(lambda one_key: jax.random.permutation(one_key, extra))(slab_keys)
    extra_rows = jnp.take_along_axis(extra_rows, orders, axis=1)
    extra_cols = jnp.take_along_axis(extra_cols, orders, axis=1)
    diagonal = jnp.broadcast_to(jnp.arange(BLK_SLAB, dtype=jnp.int32), (N_SLAB, BLK_SLAB))
    row_lists = jnp.concatenate([diagonal, extra_rows.astype(jnp.int32)], axis=1)
    col_lists = jnp.concatenate([diagonal, extra_cols.astype(jnp.int32)], axis=1)
    return (row_lists.reshape(-1), col_lists.reshape(-1))


def draw_tile_rows(key, part):
    return tile_layout(key)[0]


def draw_tile_cols(key, part):
    return tile_layout(key)[1]


def level_of(stream_key, dims, shards, least, top_value):
    def one(axis_at, parts):
        steps = jax.random.uniform(jax.random.fold_in(jax.random.fold_in(stream_key, 6), axis_at), (parts,), jnp.float32, least / len(shards), top_value / len(shards))
        return jnp.repeat(jnp.exp(steps), dims[axis_at] // parts).reshape((-1,) + (1,) * (len(dims) - axis_at - 1))

    factor_of = one(*shards[0])
    for cut in shards[1:]:
        factor_of = factor_of * one(*cut)
    return factor_of


def length_profile(number_of, total, bound, slope):
    portions = [(1 << 20) // math.isqrt(standing ** slope) + 1 for standing in range(2, number_of + 1)]
    spare, given = total - bound - (number_of - 1), [1] * (number_of - 1)
    while spare > 0:
        free = [i for i in range(number_of - 1) if given[i] < bound]
        mass, budget = sum([portions[i] for i in free]), spare
        for i in free:
            more = min(bound - given[i], max(1, budget * portions[i] // mass), spare)
            given[i] = given[i] + more
            spare = spare - more
    return np.array([bound] + given)


def ragged(key, number_of, total, bound, skew):
    if number_of == 2:
        one = jax.random.randint(key, (), max(1, total - bound), min(bound, total - 1) + 1)
        return jnp.stack([one, total - one])
    sizes = jnp.asarray(length_profile(number_of, total, bound, skew), jnp.int32)
    pairs = (number_of - 1) // 2
    giver, sink = sizes[1:1 + 2 * pairs:2], sizes[2:2 + 2 * pairs:2]
    room = jnp.minimum(giver - 1, bound - sink)
    moved = jax.random.randint(jax.random.fold_in(key, 1), (pairs,), 0, 1 << 20) % (room + 1)
    sizes = sizes.at[1:1 + 2 * pairs:2].set(giver - moved).at[2:2 + 2 * pairs:2].set(sink + moved)
    return sizes[jax.random.permutation(jax.random.fold_in(key, 2), number_of)]


def gaussian(key, dims, deviation, bound, cuts=(), kind=jnp.bfloat16):
    gain = level_of(key, dims, cuts, -0.22, 0.18) if cuts else 1.0
    drawn = jax.random.normal(key, dims, jnp.float32) * deviation * gain
    return jnp.minimum(jnp.maximum(drawn, -bound), bound).astype(kind)


def setup_inputs(seed: int = 0) -> dict:
    keys = jax.random.split(jax.random.key(seed), 8)
    orbitals_t = gaussian(keys[0], (NORB, ROWS), 1.0, 6.0, ((0, 64), (1, 8)))
    tiles = gaussian(keys[1], (N_SLAB * TILES_SLAB, TILE, TILE), (2 * TILE) ** -0.5, 0.375, ((0, 8),))
    tile_rows = draw_tile_rows(jax.random.fold_in(keys[7], 71), 0)
    tile_cols = draw_tile_cols(jax.random.fold_in(keys[7], 71), 0)
    row_counts = ragged(keys[4], NBLK, NBLK * TILE * 3 // 4, TILE, 2).astype(jnp.int32)
    bounds = jnp.clip(jax.random.uniform(keys[5], (3,), jnp.float32, 0.0, 1.0), 0.0, 1.0)
    rotation = gaussian(keys[6], (NORB, NORB), NORB ** -0.5, 0.125, ((0, 64),))
    return dict(orbitals_t=orbitals_t, tiles=tiles, tile_rows=tile_rows, tile_cols=tile_cols, row_counts=row_counts, bounds=bounds, rotation=rotation)


def tile_product(source, tiles, tile_rows, tile_cols):
    col_blocks = source.reshape(NORB, NBLK, TILE)
    col_blocks = jnp.pad(col_blocks, ((0, 0), (HB, HB), (0, 0)))
    row_lists = tile_rows.reshape(N_SLAB, TILES_SLAB)
    col_lists = tile_cols.reshape(N_SLAB, TILES_SLAB)
    slab_tiles = tiles.reshape(N_SLAB, TILES_SLAB, TILE, TILE)

    def one_slab(slab_index):
        where = slab_index * BLK_SLAB + col_lists[slab_index] + HB
        picked = jnp.take(col_blocks, where.astype(jnp.int32), axis=1).astype(jnp.float32)
        products = jnp.einsum('otc,trc->otr', picked, slab_tiles[slab_index].astype(jnp.float32))
        onehot = (row_lists[slab_index][:, None] == jnp.arange(BLK_SLAB, dtype=jnp.int32)[None, :]).astype(jnp.float32)
        return jnp.einsum('otr,tb->obr', products, onehot, precision=lax.Precision.HIGHEST)

    summed = lax.map(one_slab, jnp.arange(N_SLAB, dtype=jnp.int32))
    return jnp.transpose(summed, (1, 0, 2, 3)).reshape(NORB, ROWS)


def reference(orbitals_t, tiles, tile_rows, tile_cols, row_counts, bounds, rotation):
    lower_bound = -3.0 + bounds[0]
    cutoff = bounds[1] - 0.5
    upper_bound = 3.0 + bounds[2]
    half_width = (upper_bound - cutoff) / 2.0
    center = (upper_bound + cutoff) / 2.0
    sigma_one = half_width / (lower_bound - center)
    sigma_two = 1.0 / (2.0 / sigma_one - sigma_one)
    live = (jnp.arange(TILE, dtype=jnp.int32)[None, :] < row_counts[:, None]).astype(jnp.float32).reshape(ROWS)
    source = orbitals_t.astype(jnp.float32)
    applied = tile_product(orbitals_t, tiles, tile_rows, tile_cols)
    filtered_one = (live * (applied - center * source) * (sigma_one / half_width)).astype(jnp.bfloat16)
    applied = tile_product(filtered_one, tiles, tile_rows, tile_cols)
    first = filtered_one.astype(jnp.float32)
    filtered_two = (live * ((applied - center * first) * (2.0 * sigma_two / half_width) - sigma_one * sigma_two * source)).astype(jnp.bfloat16)
    rotated = jnp.dot(rotation.T, filtered_two, preferred_element_type=jnp.float32)
    return rotated.astype(jnp.bfloat16)
```

```python
import functools

import jax
import jax.numpy as jnp
from jax import lax
from jax.experimental import pallas as pl
from jax.experimental.pallas import tpu as pltpu
from jax.sharding import PartitionSpec as P

HB = 2
NX, NZ = 4, 8
CHIPS = NX * NZ
NORB_DEV = 32
TILE = 128
PAIR = 2 * TILE
STEPS = 4
MESH = pl.DeviceIdType.MESH
BF16 = jnp.bfloat16


def column_group(core, half, step, z):
    owner_x = 2 * core + lax.rem(step + z, 2)
    z_pair = half + 2 * lax.rem(step // 2 + z // 2, 2)
    return owner_x * 4 + z_pair


def rotate_kernel(
    f2_hbm, r_hbm, out_hbm,
    f2, rv, rb, fb, ft, ob, ov,
    in_sem, z_send, z_recv, x_send, x_recv, y_send, y_recv,
    f_send, f_recv, g_send, g_recv, o_send, o_recv, out_sem,
):
    s, o = lax.axis_index("slab"), lax.axis_index("orb")
    n_slab, n_orb = 8, 64
    core, chip = lax.rem(o, 2), o // 2
    z, x = lax.rem(chip, NZ), chip // NZ
    half = lax.rem(s, 2)
    partner = o + 1 - 2 * core
    x_up, x_down = lax.rem(x + 1, NX), lax.rem(x + NX - 1, NX)
    x_far = lax.rem(x + 2, NX)
    s_up, s_down = lax.rem(s + 1, n_slab), lax.rem(s + n_slab - 1, n_slab)

    load_r = pltpu.make_async_copy(r_hbm, rv, in_sem.at[0])
    load_r.start()
    load_f = pltpu.make_async_copy(f2_hbm, f2, in_sem.at[1])
    load_f.start()

    barrier = pltpu.get_barrier_semaphore()

    def greet(i, carry):
        pl.semaphore_signal(barrier, inc=1, device_id=(s, lax.rem(o + i, n_orb)), device_id_type=MESH)
        return carry

    lax.fori_loop(1, n_orb, greet, 0)
    for other in (s_up, s_down):
        pl.semaphore_signal(barrier, inc=1, device_id=(other, o), device_id_type=MESH)
    load_r.wait()
    load_f.wait()
    pl.semaphore_wait(barrier, n_orb - 1 + 2)

    def send(src, dst, send_sem, recv_sem, to):
        pltpu.make_async_remote_copy(
            src_ref=src, dst_ref=dst, send_sem=send_sem, recv_sem=recv_sem,
            device_id=to, device_id_type=MESH,
        ).start()

    def wait_bytes(ref, sem):
        pltpu.make_async_copy(ref, ref, sem).wait()

    def rotation_columns(to_core, step, to_z):
        first = column_group(to_core, half, step, to_z) * TILE
        return rv.at[:, pl.ds(pl.multiple_of(first, TILE), TILE)]

    def z_step(step, carry):
        pltpu.make_async_copy(
            rotation_columns(core, step, z), rb.at[half, step, core, chip], z_recv.at[step]
        ).start()

        def one(i, inner):
            there = lax.rem(z * 2 + core + i, 2 * NZ)
            send(
                rotation_columns(lax.rem(there, 2), step, there // 2),
                rb.at[half, step, core, chip], z_send, z_recv.at[step], (s, x * 2 * NZ + there),
            )
            return inner

        lax.fori_loop(1, 2 * NZ, one, 0)
        return carry

    lax.fori_loop(0, STEPS, z_step, 0)

    pltpu.make_async_copy(
        f2.at[:, pl.ds(pl.multiple_of(chip * PAIR, PAIR), PAIR)], fb.at[core, chip], f_recv.at[x]
    ).start()

    def f_one(i, carry):
        there = lax.rem(chip + i, CHIPS)
        send(
            f2.at[:, pl.ds(pl.multiple_of(there * PAIR, PAIR), PAIR)],
            fb.at[core, chip], f_send, f_recv.at[x], (s, there * 2 + core),
        )
        return carry

    lax.fori_loop(1, CHIPS, f_one, 0)

    def of_x(step, which, at_x):
        return rb.at[which, step, :, pl.ds(at_x * NZ, NZ)]

    def of_x_core(step, which, at_core, at_x):
        return rb.at[which, step, at_core, pl.ds(at_x * NZ, NZ)]

    def to_slabs(step, at_x):
        send(of_x_core(step, half, 0, at_x), of_x_core(step, half, 0, at_x), y_send, y_recv.at[step], (s_up, o))
        send(of_x_core(step, half, 1, at_x), of_x_core(step, half, 1, at_x), y_send, y_recv.at[step], (s_down, o))

    def orb_at(at_x):
        return (at_x * NZ + z) * 2 + core

    def stage_one(step, carry):
        mine = of_x(step, half, x)
        wait_bytes(mine, z_recv.at[step])
        send(mine, mine, x_send, x_recv.at[step, 0], (s, orb_at(x_up)))
        send(mine, mine, x_send, x_recv.at[step, 1], (s, orb_at(x_down)))
        to_slabs(step, x)
        return carry

    def stage_two(step, carry):
        wait_bytes(of_x(step, half, x_down), x_recv.at[step, 0])
        relayed = of_x_core(step, half, 0, x_down)
        send(relayed, relayed, x_send, x_recv.at[step, 2], (s, orb_at(x_up)))
        wait_bytes(of_x(step, half, x_up), x_recv.at[step, 1])
        relayed = of_x_core(step, half, 1, x_up)
        send(relayed, relayed, x_send, x_recv.at[step, 3], (s, orb_at(x_down)))
        to_slabs(step, x_down)
        to_slabs(step, x_up)
        return carry

    def stage_three(step, carry):
        wait_bytes(of_x_core(step, half, 0, x_far), x_recv.at[step, 2])
        wait_bytes(of_x_core(step, half, 1, x_far), x_recv.at[step, 3])
        to_slabs(step, x_far)
        return carry

    lax.fori_loop(0, STEPS, stage_one, 0)
    lax.fori_loop(0, STEPS, stage_two, 0)

    def pass_on(at_x, carry):
        got = fb.at[core, pl.ds(at_x * NZ, NZ)]
        wait_bytes(got, f_recv.at[at_x])
        send(got, got, g_send, g_recv.at[at_x], (s, partner))
        return carry

    lax.fori_loop(0, NX, pass_on, 0)
    lax.fori_loop(0, STEPS, stage_three, 0)

    def wait_partner(at_x, carry):
        wait_bytes(fb.at[1 - core, pl.ds(at_x * NZ, NZ)], g_recv.at[at_x])
        return carry

    lax.fori_loop(0, NX, wait_partner, 0)

    for at_core in range(2):
        for group in range(CHIPS // 4):
            block = fb[at_core, 4 * group:4 * group + 4].reshape(TILE, PAIR)
            first = at_core * CHIPS * NORB_DEV + group * TILE
            ft[:, first:first + TILE] = block.T

    def rotate(step, which):
        slot = rb[which, step].reshape(2 * CHIPS * NORB_DEV, TILE)
        made = jnp.dot(ft[...], slot, preferred_element_type=jnp.float32)
        ob[which, step] = made.T.astype(BF16)
        first = column_group(core, which, step, z) * 4
        columns = pl.ds(pl.multiple_of(chip * PAIR, PAIR), PAIR)
        for i in range(4):
            piece = ob.at[which, step, pl.ds(i * NORB_DEV, NORB_DEV)]

            @pl.when(first + i == o)
            def _():
                pltpu.make_async_copy(piece, ov.at[:, columns], o_recv).start()

            @pl.when(first + i != o)
            def _():
                send(piece, ov.at[:, columns], o_send, o_recv, (s, first + i))

    def finish(step, carry):
        rotate(step, half)
        wait_bytes(rb.at[1 - half, step], y_recv.at[step])
        rotate(step, 1 - half)
        return carry

    lax.fori_loop(0, STEPS, finish, 0)

    wait_bytes(ov, o_recv)
    store = pltpu.make_async_copy(ov, out_hbm, out_sem)
    store.start()
    wait_bytes(rb.at[0, 0, :, pl.ds(0, 30)], z_send)
    wait_bytes(rb.at[0, pl.ds(0, 3)], x_send)
    wait_bytes(rb.at[0], y_send)
    wait_bytes(fb.at[0, pl.ds(0, CHIPS - 1)], f_send)
    wait_bytes(fb.at[0], g_send)

    @pl.when(x // 2 == core)
    def _():
        wait_bytes(fb.at[0, pl.ds(0, CHIPS - 1)], o_send)

    @pl.when(x // 2 != core)
    def _():
        wait_bytes(fb.at[0], o_send)

    store.wait()


def rotate(filtered, rotation):
    rows = filtered.shape[1]
    dma = pltpu.SemaphoreType.DMA
    return pl.pallas_call(
        rotate_kernel,
        out_shape=jax.ShapeDtypeStruct(filtered.shape, BF16),
        in_specs=[pl.BlockSpec(memory_space=pl.ANY)] * 2,
        out_specs=pl.BlockSpec(memory_space=pl.ANY),
        scratch_shapes=[
            pltpu.VMEM((NORB_DEV, rows), BF16),
            pltpu.VMEM(rotation.shape, BF16),
            pltpu.VMEM((2, STEPS, 2, CHIPS, NORB_DEV, TILE), BF16),
            pltpu.VMEM((2, CHIPS, NORB_DEV, PAIR), BF16),
            pltpu.VMEM((PAIR, 2 * CHIPS * NORB_DEV), BF16),
            pltpu.VMEM((2, STEPS, TILE, PAIR), BF16),
            pltpu.VMEM((NORB_DEV, rows), BF16),
            dma((2,)), dma, dma((STEPS,)), dma, dma((STEPS, 4)), dma, dma((STEPS,)),
            dma, dma((NX,)), dma, dma((NX,)), dma, dma, dma,
        ],
        compiler_params=pltpu.CompilerParams(
            collective_id=0, has_side_effects=True, vmem_limit_bytes=40 << 20
        ),
    )(filtered, rotation)


def with_halo(block, sides, width):
    for axis, dim in sides:
        count = lax.axis_size(axis)
        forward = [(i, i + 1) for i in range(count - 1)]
        backward = [(target, source) for source, target in forward]
        low = lax.ppermute(
            lax.slice_in_dim(block, block.shape[dim] - width, None, axis=dim), axis, forward
        )
        high = lax.ppermute(lax.slice_in_dim(block, 0, width, axis=dim), axis, backward)
        block = jnp.concatenate([low, block, high], axis=dim)
    return block


def local(orbitals_t, tiles, tile_rows, tile_cols, row_counts, bounds, rotation):
    norb_dev, rows_dev = orbitals_t.shape
    tile_size = tiles.shape[1]
    blocks = rows_dev // tile_size
    lower_bound = -3.0 + bounds[0]
    cutoff = bounds[1] - 0.5
    upper_bound = 3.0 + bounds[2]
    half_width = (upper_bound - cutoff) / 2.0
    center = (upper_bound + cutoff) / 2.0
    sigma_one = half_width / (lower_bound - center)
    sigma_two = 1.0 / (2.0 / sigma_one - sigma_one)
    live = (
        (lax.broadcasted_iota(jnp.int32, (blocks, tile_size), 1) < row_counts[:, None])
        .astype(jnp.float32)
        .reshape(rows_dev)
    )
    extra_rows = tile_rows[blocks:]
    onehot = (extra_rows[:, None] == lax.broadcasted_iota(jnp.int32, (1, blocks), 1)).astype(
        jnp.float32
    )
    col_index = tile_cols + HB

    def apply_tiles(source):
        extended = with_halo(source, (("slab", 1),), HB * tile_size)
        col_blocks = extended.reshape(norb_dev, blocks + 2 * HB, tile_size)
        picked = jnp.take(col_blocks, col_index, axis=1)
        products = jnp.einsum("otc,trc->otr", picked, tiles, preferred_element_type=jnp.float32)
        diagonal_part = products[:, :blocks]
        extra_part = jnp.einsum(
            "otr,tb->obr", products[:, blocks:], onehot, precision=lax.Precision.HIGH
        )
        summed = diagonal_part + extra_part
        return summed.reshape(norb_dev, rows_dev)

    source = orbitals_t.astype(jnp.float32)
    applied = apply_tiles(orbitals_t)
    filtered_one = (live * (applied - center * source) * (sigma_one / half_width)).astype(
        jnp.bfloat16
    )
    applied = apply_tiles(filtered_one)
    first = filtered_one.astype(jnp.float32)
    filtered_two = (
        live
        * (
            (applied - center * first) * (2.0 * sigma_two / half_width)
            - sigma_one * sigma_two * source
        )
    ).astype(jnp.bfloat16)
    return rotate(filtered_two, rotation)


def solution(mesh):
    return jax.shard_map(
        local,
        mesh=mesh,
        in_specs=(
            P("orb", "slab"),
            P("slab", None, None),
            P("slab"),
            P("slab"),
            P("slab"),
            P(),
            P("orb", None),
        ),
        out_specs=P("orb", "slab"),
        check_vma=False,
    )
```

```python
import jax
import jax.numpy as jnp
from jax import lax
from jax.experimental import pallas as pl
from jax.experimental.pallas import tpu as pltpu
from jax.sharding import PartitionSpec as P

HB = 2
NX, NZ = 4, 8
CHIPS = NX * NZ
N_SLAB = 8
N_ORB = 2 * CHIPS
NORB_DEV = 32
TILE = 128
PAIR = 2 * TILE
BLOCKS = 64
EXTRA = 48
COL, WHICH, GOES_ON, LAST, LIVE, ENTRIES = 0, 48, 96, 144, 208, 272
ROWS_DEV = BLOCKS * TILE
STEPS = 4
UNROLL = 8
MESH = pl.DeviceIdType.MESH
BF16, F32 = jnp.bfloat16, jnp.float32


def column_group(core, half, step, z):
    owner_x = 2 * core + lax.rem(step + z, 2)
    z_pair = half + 2 * lax.rem(step // 2 + z // 2, 2)
    return owner_x * 4 + z_pair


def aligned(index, size):
    return pl.ds(pl.multiple_of(index * size, size), size)


def kernel(
    table_hbm, bounds_hbm, orb_hbm, tiles_hbm, r_hbm, out_hbm,
    table, bounds, e0, e1, diag, extra, acc, seg, coef, f2, rv, rb, fb, ft, ob, ov,
    in_sem, h_send, h_recv, z_send, z_recv, x_send, x_recv,
    f_send, f_recv, g_send, g_recv, o_send, o_recv, out_sem,
):
    s, o = lax.axis_index("slab"), lax.axis_index("orb")
    core, chip = lax.rem(o, 2), o // 2
    z, x = lax.rem(chip, NZ), chip // NZ
    half = lax.rem(s, 2)
    partner = o + 1 - 2 * core
    x_up, x_down = lax.rem(x + 1, NX), lax.rem(x + NX - 1, NX)
    x_far = lax.rem(x + 2, NX)
    s_up, s_down = lax.rem(s + 1, N_SLAB), lax.rem(s + N_SLAB - 1, N_SLAB)
    not_first, not_last = s > 0, s < N_SLAB - 1

    loads = [
        pltpu.make_async_copy(table_hbm, table, in_sem.at[0]),
        pltpu.make_async_copy(bounds_hbm, bounds, in_sem.at[4]),
        pltpu.make_async_copy(r_hbm, rv, in_sem.at[1]),
        pltpu.make_async_copy(tiles_hbm.at[pl.ds(0, BLOCKS)], diag, in_sem.at[2]),
        pltpu.make_async_copy(tiles_hbm.at[pl.ds(BLOCKS, EXTRA)], extra, in_sem.at[3]),
    ]
    for load in loads:
        load.start()

    def load_block(b, carry):
        pltpu.make_async_copy(orb_hbm.at[:, aligned(b, TILE)], e0.at[HB + b], in_sem.at[5]).start()
        return carry

    lax.fori_loop(0, BLOCKS, load_block, 0)

    def wait_bytes(ref, sem):
        pltpu.make_async_copy(ref, ref, sem).wait()

    barrier = pltpu.get_barrier_semaphore()

    def greet(i, carry):
        there = lax.rem(o + i, N_ORB)

        @pl.when(i > 0)
        def _():
            pl.semaphore_signal(barrier, inc=1, device_id=(s, there), device_id_type=MESH)

        for other in (s_up, s_down):
            pl.semaphore_signal(barrier, inc=1, device_id=(other, there), device_id_type=MESH)
        return carry

    lax.fori_loop(0, N_ORB, greet, 0)

    loads[0].wait()
    loads[1].wait()
    lower = jnp.full((8, TILE), bounds[0]) - 3.0
    cutoff = jnp.full((8, TILE), bounds[1]) - 0.5
    upper = jnp.full((8, TILE), bounds[2]) + 3.0
    half_width = (upper - cutoff) / 2.0
    center = (upper + cutoff) / 2.0
    sigma_one = half_width / (lower - center)
    sigma_two = 1.0 / (2.0 / sigma_one - sigma_one)
    coef[0] = center
    coef[1] = sigma_one / half_width
    coef[2] = 2.0 * sigma_two / half_width
    coef[3] = sigma_one * sigma_two

    for ext in (e0, e1):
        @pl.when(s == 0)
        def _():
            ext[:HB] = jnp.zeros((HB, NORB_DEV, TILE), BF16)

        @pl.when(s == N_SLAB - 1)
        def _():
            ext[HB + BLOCKS:] = jnp.zeros((HB, NORB_DEV, TILE), BF16)

    seg[EXTRA] = jnp.zeros((NORB_DEV, TILE), F32)

    loads[2].wait()
    wait_bytes(e0.at[pl.ds(HB, BLOCKS)], in_sem.at[5])
    pl.semaphore_wait(barrier, 3 * N_ORB - 1)

    def send(src, dst, send_sem, recv_sem, to):
        pltpu.make_async_remote_copy(
            src_ref=src, dst_ref=dst, send_sem=send_sem, recv_sem=recv_sem,
            device_id=to, device_id_type=MESH,
        ).start()

    low_edge, high_edge = pl.ds(0, HB), pl.ds(HB + BLOCKS, HB)

    def send_edges(ext, which):
        @pl.when(not_last)
        def _():
            send(ext.at[pl.ds(BLOCKS, HB)], ext.at[low_edge],
                 h_send.at[which, 0], h_recv.at[which, 0], (s_up, o))

        @pl.when(not_first)
        def _():
            send(ext.at[pl.ds(HB, HB)], ext.at[high_edge],
                 h_send.at[which, 1], h_recv.at[which, 1], (s_down, o))

    def wait_edges(ext, which):
        @pl.when(not_first)
        def _():
            wait_bytes(ext.at[low_edge], h_recv.at[which, 0])

        @pl.when(not_last)
        def _():
            wait_bytes(ext.at[high_edge], h_recv.at[which, 1])

    send_edges(e0, 0)

    def rotation_columns(to_core, step, to_z):
        return rv.at[:, aligned(column_group(to_core, half, step, to_z), TILE)]

    def z_step(step, carry):
        pltpu.make_async_copy(
            rotation_columns(core, step, z), rb.at[step, core, chip], z_recv.at[step]
        ).start()

        def one(i, inner):
            there = lax.rem(z * 2 + core + i, 2 * NZ)
            send(
                rotation_columns(lax.rem(there, 2), step, there // 2),
                rb.at[step, core, chip], z_send, z_recv.at[step], (s, x * 2 * NZ + there),
            )
            return inner

        lax.fori_loop(1, 2 * NZ, one, 0)
        return carry

    lax.fori_loop(0, STEPS, z_step, 0)

    def of_x(step, at_x):
        return rb.at[step, :, pl.ds(at_x * NZ, NZ)]

    def of_x_core(step, at_core, at_x):
        return rb.at[step, at_core, pl.ds(at_x * NZ, NZ)]

    def orb_at(at_x):
        return (at_x * NZ + z) * 2 + core

    def stage_one(step):
        mine = of_x(step, x)
        wait_bytes(mine, z_recv.at[step])
        send(mine, mine, x_send, x_recv.at[step, 0], (s, orb_at(x_up)))
        send(mine, mine, x_send, x_recv.at[step, 1], (s, orb_at(x_down)))

    def stage_two(step):
        wait_bytes(of_x(step, x_down), x_recv.at[step, 0])
        relayed = of_x_core(step, 0, x_down)
        send(relayed, relayed, x_send, x_recv.at[step, 2], (s, orb_at(x_up)))
        wait_bytes(of_x(step, x_up), x_recv.at[step, 1])
        relayed = of_x_core(step, 1, x_up)
        send(relayed, relayed, x_send, x_recv.at[step, 3], (s, orb_at(x_down)))

    def stage_three(step):
        wait_bytes(of_x_core(step, 0, x_far), x_recv.at[step, 2])
        wait_bytes(of_x_core(step, 1, x_far), x_recv.at[step, 3])

    def times_tile(rows, tile):
        return lax.dot_general(rows, tile, (((1,), (1,)), ((), ())), preferred_element_type=F32)

    def apply_diagonal(ext):
        def body(i, carry):
            for u in range(UNROLL):
                b = i * UNROLL + u
                acc[b] = times_tile(ext[b + HB], diag[b])
            return carry

        lax.fori_loop(0, BLOCKS // UNROLL, body, 0)

    def apply_extra(ext):
        def multiply(i, carry):
            for u in range(UNROLL):
                m = i * UNROLL + u
                seg[m] = times_tile(ext[table[COL + m]], extra[table[WHICH + m]])
            return carry

        lax.fori_loop(0, EXTRA // UNROLL, multiply, 0)

        def add_up(i, run):
            for u in range(UNROLL):
                m = i * UNROLL + u
                run = seg[m] + table[GOES_ON + m].astype(F32) * run
                seg[m] = run
            return run

        lax.fori_loop(0, EXTRA // UNROLL, add_up, jnp.zeros((NORB_DEV, TILE), F32))

    lanes = lax.broadcasted_iota(jnp.int32, (1, TILE), 1)

    def filtered_first(b):
        total = acc[b] + seg[table[LAST + b]]
        source = e0[b + HB].astype(F32)
        value = (total - coef[0, 0:1] * source) * coef[1, 0:1]
        e1[b + HB] = jnp.where(lanes < table[LIVE + b], value, 0.0).astype(BF16)

    def filtered_second(b):
        total = acc[b] + seg[table[LAST + b]]
        source = e0[b + HB].astype(F32)
        first = e1[b + HB].astype(F32)
        value = (total - coef[0, 0:1] * first) * coef[2, 0:1] - coef[3, 0:1] * source
        return jnp.where(lanes < table[LIVE + b], value, 0.0).astype(BF16)

    loads[3].wait()
    apply_diagonal(e0)
    loads[4].wait()
    wait_edges(e0, 0)
    apply_extra(e0)
    for b in (0, 1, BLOCKS - 2, BLOCKS - 1):
        filtered_first(b)
    send_edges(e1, 1)

    def inner_first(i, carry):
        for u in range(4):
            filtered_first(HB + 4 * i + u)
        return carry

    lax.fori_loop(0, (BLOCKS - 2 * HB) // 4, inner_first, 0)
    apply_diagonal(e1)
    stage_one(0)
    wait_edges(e1, 1)
    apply_extra(e1)
    stage_one(1)

    def destination(i):
        return lax.rem(x + i // NZ, NX) * NZ + lax.rem(z + lax.rem(i, NZ), NZ)

    def f_one(i, carry):
        there = destination(i)
        f2[there, :, :TILE] = filtered_second(2 * there)
        f2[there, :, TILE:] = filtered_second(2 * there + 1)

        @pl.when(i > 0)
        def _():
            send(f2.at[there], fb.at[core, chip, :, pl.ds(0, PAIR)], f_send, f_recv.at[x], (s, there * 2 + core))

        @pl.when(i == 0)
        def _():
            pltpu.make_async_copy(f2.at[there], fb.at[core, chip, :, pl.ds(0, PAIR)], f_recv.at[x]).start()

        return carry

    lax.fori_loop(0, CHIPS, f_one, 0)

    def turn(at_core, at_x, first_row):
        for group in range(2):
            block = fb[at_core, pl.ds(at_x * NZ + 4 * group, 4), :, first_row:first_row + TILE]
            k = at_core * (CHIPS * NORB_DEV) + (at_x * 2 + group) * TILE
            ft[first_row:first_row + TILE, aligned(k // TILE, TILE)] = block.reshape(TILE, TILE).T

    def pass_on(at_x):
        at = pl.ds(at_x * NZ, NZ)
        got = fb.at[core, at, :, pl.ds(0, PAIR)]
        wait_bytes(got, f_recv.at[at_x])
        for to in (o, partner):
            send(fb.at[core, at, :, pl.ds(0, TILE)], fb.at[core, at, :, pl.ds(PAIR, TILE)],
                 g_send, g_recv.at[at_x, 1], (s_up, to))
            send(fb.at[core, at, :, pl.ds(TILE, TILE)], fb.at[core, at, :, pl.ds(PAIR + TILE, TILE)],
                 g_send, g_recv.at[at_x, 2], (s_down, to))
        send(got, got, g_send, g_recv.at[at_x, 0], (s, partner))
        turn(core, at_x, 0)
        turn(core, at_x, TILE)

    def take(at_x):
        at = pl.ds(at_x * NZ, NZ)
        wait_bytes(fb.at[1 - core, at, :, pl.ds(0, PAIR)], g_recv.at[at_x, 0])
        turn(1 - core, at_x, 0)
        turn(1 - core, at_x, TILE)
        for side in range(2):
            wait_bytes(fb.at[:, at, :, pl.ds(PAIR + side * TILE, TILE)], g_recv.at[at_x, 1 + side])
            turn(0, at_x, PAIR + side * TILE)
            turn(1, at_x, PAIR + side * TILE)

    def back_x(i):
        return lax.rem(x + NX - i, NX)

    stage_one(2)
    stage_one(3)
    stage_two(0)
    stage_two(1)
    pass_on(back_x(0))
    stage_three(0)
    stage_two(2)
    pass_on(back_x(1))
    stage_three(1)
    stage_two(3)
    pass_on(back_x(2))
    stage_three(2)
    pass_on(back_x(3))
    for i in range(NX):
        take(back_x(i))
    stage_three(3)

    def rotate(step, carry):
        slot = rb[step].reshape(2 * CHIPS * NORB_DEV, TILE)
        made = jnp.dot(ft[...], slot, preferred_element_type=F32)
        ob[step] = made.T.astype(BF16)
        first = column_group(core, half, step, z) * 4
        own = pl.ds(pl.multiple_of(chip * PAIR, PAIR), PAIR)
        low = pl.ds(pl.multiple_of(chip * PAIR, TILE), TILE)
        high = pl.ds(pl.multiple_of(chip * PAIR + TILE, TILE), TILE)
        for i in range(4):
            rows = pl.ds(i * NORB_DEV, NORB_DEV)
            owner = first + i
            send(ob.at[step, rows, pl.ds(PAIR, TILE)], ov.at[:, low], o_send, o_recv, (s_down, owner))
            send(ob.at[step, rows, pl.ds(PAIR + TILE, TILE)], ov.at[:, high], o_send, o_recv, (s_up, owner))
            piece = ob.at[step, rows, pl.ds(0, PAIR)]

            @pl.when(owner == o)
            def _():
                pltpu.make_async_copy(piece, ov.at[:, own], o_recv).start()

            @pl.when(owner != o)
            def _():
                send(piece, ov.at[:, own], o_send, o_recv, (s, owner))

        return carry

    lax.fori_loop(0, STEPS, rotate, 0)

    wait_bytes(ov, o_recv)
    store = pltpu.make_async_copy(ov, out_hbm, out_sem)
    store.start()
    for which, ext in ((0, e0), (1, e1)):
        @pl.when(not_last)
        def _():
            wait_bytes(ext.at[low_edge], h_send.at[which, 0])

        @pl.when(not_first)
        def _():
            wait_bytes(ext.at[high_edge], h_send.at[which, 1])

    wait_bytes(rb.at[0, :, pl.ds(0, 30)], z_send)
    wait_bytes(rb.at[pl.ds(0, 3)], x_send)
    wait_bytes(f2.at[pl.ds(0, CHIPS - 1)], f_send)
    wait_bytes(fb.at[:, :, :, pl.ds(0, PAIR + TILE)], g_send)
    mine_too = (x // 2 == core) & (lax.rem(z // 2, 2) == half)

    @pl.when(mine_too)
    def _():
        wait_bytes(f2.at[pl.ds(0, CHIPS - 1)], o_send)

    @pl.when(jnp.logical_not(mine_too))
    def _():
        wait_bytes(f2, o_send)

    store.wait()


def small_table(tile_rows, tile_cols, row_counts):
    rows, cols = tile_rows[BLOCKS:], tile_cols[BLOCKS:] + HB
    count = jnp.arange(EXTRA, dtype=jnp.int32)
    same_before = (rows[None, :] == rows[:, None]) & (count[None, :] < count[:, None])
    place = jnp.sum(((rows[None, :] < rows[:, None]) | same_before).astype(jnp.int32), axis=1)
    goes_on = jnp.max(same_before.astype(jnp.int32), axis=1)
    def in_order(values):
        return jnp.sum(jnp.where(place[None, :] == count[:, None], values[None, :], 0), axis=1)

    block = jnp.arange(BLOCKS, dtype=jnp.int32)
    up_to = jnp.sum((rows[None, :] <= block[:, None]).astype(jnp.int32), axis=1)
    any_tile = jnp.any(rows[None, :] == block[:, None], axis=1)
    return jnp.concatenate([in_order(cols), in_order(count), in_order(goes_on), jnp.where(any_tile, up_to - 1, EXTRA), row_counts])


def local(orbitals_t, tiles, tile_rows, tile_cols, row_counts, bounds, rotation):
    dma = pltpu.SemaphoreType.DMA
    ext = pltpu.VMEM((BLOCKS + 2 * HB, NORB_DEV, TILE), BF16)
    anywhere = pl.BlockSpec(memory_space=pl.ANY)
    return pl.pallas_call(
        kernel,
        out_shape=jax.ShapeDtypeStruct(orbitals_t.shape, BF16),
        in_specs=[anywhere] * 5,
        out_specs=anywhere,
        scratch_shapes=[
            pltpu.SMEM((ENTRIES,), jnp.int32),
            pltpu.SMEM((3,), F32),
            ext, ext,
            pltpu.VMEM((BLOCKS, TILE, TILE), BF16),
            pltpu.VMEM((EXTRA, TILE, TILE), BF16),
            pltpu.VMEM((BLOCKS, NORB_DEV, TILE), F32),
            pltpu.VMEM((EXTRA + 1, NORB_DEV, TILE), F32),
            pltpu.VMEM((4, 8, TILE), F32),
            pltpu.VMEM((CHIPS, NORB_DEV, PAIR), BF16),
            pltpu.VMEM((NORB_DEV, N_ORB * NORB_DEV), BF16),
            pltpu.VMEM((STEPS, 2, CHIPS, NORB_DEV, TILE), BF16),
            pltpu.VMEM((2, CHIPS, NORB_DEV, 2 * PAIR), BF16),
            pltpu.VMEM((2 * PAIR, N_ORB * NORB_DEV), BF16),
            pltpu.VMEM((STEPS, TILE, 2 * PAIR), BF16),
            pltpu.VMEM((NORB_DEV, ROWS_DEV), BF16),
            dma((6,)), dma((2, 2)), dma((2, 2)), dma, dma((STEPS,)), dma, dma((STEPS, 4)),
            dma, dma((NX,)), dma, dma((NX, 3)), dma, dma, dma,
        ],
        compiler_params=pltpu.CompilerParams(
            collective_id=0, has_side_effects=True, vmem_limit_bytes=40 << 20
        ),
    )(small_table(tile_rows, tile_cols, row_counts), bounds, orbitals_t, tiles, rotation)


def solution(mesh):
    return jax.shard_map(
        local,
        mesh=mesh,
        in_specs=(
            P("orb", "slab"),
            P("slab", None, None),
            P("slab"),
            P("slab"),
            P("slab"),
            P(),
            P("orb", None),
        ),
        out_specs=P("orb", "slab"),
        check_vma=False,
    )
```

```python
import jax
import jax.numpy as jnp
from jax import lax
from jax.experimental import pallas as pl
from jax.experimental.pallas import tpu as pltpu
from jax.sharding import PartitionSpec as P

HB = 2
NX, NZ = 4, 8
CHIPS = NX * NZ
N_SLAB = 8
N_ORB = 2 * CHIPS
NORB_DEV = 32
TILE = 128
PAIR = 2 * TILE
BLOCKS = 64
EXTRA = 48
TILES = BLOCKS + EXTRA
ROWS_DEV = BLOCKS * TILE
STEPS = 4
UNROLL = 8
MESH = pl.DeviceIdType.MESH
BF16, F32 = jnp.bfloat16, jnp.float32


def column_group(core, half, step, z):
    owner_x = 2 * core + lax.rem(step + z, 2)
    z_pair = half + 2 * lax.rem(step // 2 + z // 2, 2)
    return owner_x * 4 + z_pair


def aligned(index, size):
    return pl.ds(pl.multiple_of(index * size, size), size)


def kernel(
    rows_hbm, cols_hbm, counts_hbm, bounds_hbm, orb_hbm, tiles_hbm, r_hbm, out_hbm,
    t_rows, t_cols, t_made, col_at, which_at, goes_on_at, last_at, counts, bounds, e0, e1, diag, extra, acc, seg, coef, f2, rv, rb, fb, ft, ob, ov,
    in_sem, t_sem, h_send, h_recv, z_send, z_recv, x_send, x_recv,
    f_send, f_recv, g_send, g_recv, o_send, o_recv, out_sem,
):
    s, o = lax.axis_index("slab"), lax.axis_index("orb")
    core, chip = lax.rem(o, 2), o // 2
    z, x = lax.rem(chip, NZ), chip // NZ
    half = lax.rem(s, 2)
    partner = o + 1 - 2 * core
    x_up, x_down = lax.rem(x + 1, NX), lax.rem(x + NX - 1, NX)
    x_far = lax.rem(x + 2, NX)
    s_up, s_down = lax.rem(s + 1, N_SLAB), lax.rem(s + N_SLAB - 1, N_SLAB)
    not_first, not_last = s > 0, s < N_SLAB - 1

    loads = [
        pltpu.make_async_copy(rows_hbm, t_rows, in_sem.at[0]),
        pltpu.make_async_copy(bounds_hbm, bounds, in_sem.at[4]),
        pltpu.make_async_copy(r_hbm, rv, in_sem.at[1]),
        pltpu.make_async_copy(tiles_hbm.at[pl.ds(0, BLOCKS)], diag, in_sem.at[2]),
        pltpu.make_async_copy(tiles_hbm.at[pl.ds(BLOCKS, EXTRA)], extra, in_sem.at[3]),
        pltpu.make_async_copy(cols_hbm, t_cols, in_sem.at[6]),
        pltpu.make_async_copy(counts_hbm, counts, in_sem.at[7]),
    ]
    for load in loads:
        load.start()

    def load_block(b, carry):
        pltpu.make_async_copy(orb_hbm.at[:, aligned(b, TILE)], e0.at[HB + b], in_sem.at[5]).start()
        return carry

    lax.fori_loop(0, BLOCKS, load_block, 0)

    def wait_bytes(ref, sem):
        pltpu.make_async_copy(ref, ref, sem).wait()

    barrier = pltpu.get_barrier_semaphore()

    same_parity = lax.rem(z // 2, 2) == half

    def signal(to):
        pl.semaphore_signal(barrier, inc=1, device_id=to, device_id_type=MESH)

    def greet_chip(i, carry):
        signal((s, lax.rem(chip + i, CHIPS) * 2 + core))
        return carry

    def greet_column(i, carry):
        signal((s, (x * NZ + i) * 2 + 1 - core))
        return carry

    def greet_other(i, carry):
        signal((s, lax.rem(chip + i, CHIPS) * 2 + 1 - core))
        return carry

    def greet_near(i, carry):
        for near in (s_up, s_down):
            signal((near, lax.rem(chip + i, CHIPS) * 2 + x // 2))
        return carry

    for near in (s_up, s_down):
        for to in (o, partner):
            signal((near, to))
    lax.fori_loop(1, CHIPS, greet_chip, 0)
    lax.fori_loop(0, NZ, greet_column, 0)
    lax.fori_loop(0, jnp.where(same_parity & (core != x // 2), CHIPS, 0), greet_other, 0)
    lax.fori_loop(0, jnp.where(same_parity, 0, CHIPS), greet_near, 0)

    loads[1].wait()
    lower = jnp.full((8, TILE), bounds[0]) - 3.0
    cutoff = jnp.full((8, TILE), bounds[1]) - 0.5
    upper = jnp.full((8, TILE), bounds[2]) + 3.0
    half_width = (upper - cutoff) / 2.0
    center = (upper + cutoff) / 2.0
    sigma_one = half_width / (lower - center)
    sigma_two = 1.0 / (2.0 / sigma_one - sigma_one)
    coef[0] = center
    coef[1] = sigma_one / half_width
    coef[2] = 2.0 * sigma_two / half_width
    coef[3] = sigma_one * sigma_two

    for ext in (e0, e1):
        @pl.when(s == 0)
        def _():
            ext[:HB] = jnp.zeros((HB, NORB_DEV, TILE), BF16)

        @pl.when(s == N_SLAB - 1)
        def _():
            ext[HB + BLOCKS:] = jnp.zeros((HB, NORB_DEV, TILE), BF16)

    seg[EXTRA] = jnp.zeros((NORB_DEV, TILE), F32)

    loads[2].wait()
    wait_bytes(e0.at[pl.ds(HB, BLOCKS)], in_sem.at[5])
    pl.semaphore_wait(barrier, 4 + (CHIPS - 1) + NZ + 8 + 32)

    def send(src, dst, send_sem, recv_sem, to):
        pltpu.make_async_remote_copy(
            src_ref=src, dst_ref=dst, send_sem=send_sem, recv_sem=recv_sem,
            device_id=to, device_id_type=MESH,
        ).start()

    low_edge, high_edge = pl.ds(0, HB), pl.ds(HB + BLOCKS, HB)

    def send_edges(ext, which):
        @pl.when(not_last)
        def _():
            send(ext.at[pl.ds(BLOCKS, HB)], ext.at[low_edge],
                 h_send.at[which, 0], h_recv.at[which, 0], (s_up, o))

        @pl.when(not_first)
        def _():
            send(ext.at[pl.ds(HB, HB)], ext.at[high_edge],
                 h_send.at[which, 1], h_recv.at[which, 1], (s_down, o))

    def wait_edges(ext, which):
        @pl.when(not_first)
        def _():
            wait_bytes(ext.at[low_edge], h_recv.at[which, 0])

        @pl.when(not_last)
        def _():
            wait_bytes(ext.at[high_edge], h_recv.at[which, 1])

    send_edges(e0, 0)

    def rotation_columns(to_core, step, to_z):
        return rv.at[:, aligned(column_group(to_core, half, step, to_z), TILE)]

    def z_step(step, carry):
        pltpu.make_async_copy(
            rotation_columns(core, step, z), rb.at[step, core, chip], z_recv.at[step]
        ).start()

        def one(i, inner):
            there = lax.rem(z * 2 + core + i, 2 * NZ)
            send(
                rotation_columns(lax.rem(there, 2), step, there // 2),
                rb.at[step, core, chip], z_send, z_recv.at[step], (s, x * 2 * NZ + there),
            )
            return inner

        lax.fori_loop(1, 2 * NZ, one, 0)
        return carry

    lax.fori_loop(0, STEPS, z_step, 0)

    def of_x(step, at_x):
        return rb.at[step, :, pl.ds(at_x * NZ, NZ)]

    def of_x_core(step, at_core, at_x):
        return rb.at[step, at_core, pl.ds(at_x * NZ, NZ)]

    def orb_at(at_x):
        return (at_x * NZ + z) * 2 + core

    def stage_one(step):
        mine = of_x(step, x)
        wait_bytes(mine, z_recv.at[step])
        send(mine, mine, x_send, x_recv.at[step, 0], (s, orb_at(x_up)))
        send(mine, mine, x_send, x_recv.at[step, 1], (s, orb_at(x_down)))

    def stage_two(step):
        wait_bytes(of_x(step, x_down), x_recv.at[step, 0])
        relayed = of_x_core(step, 0, x_down)
        send(relayed, relayed, x_send, x_recv.at[step, 2], (s, orb_at(x_up)))
        wait_bytes(of_x(step, x_up), x_recv.at[step, 1])
        relayed = of_x_core(step, 1, x_up)
        send(relayed, relayed, x_send, x_recv.at[step, 3], (s, orb_at(x_down)))

    def stage_three(step):
        wait_bytes(of_x_core(step, 0, x_far), x_recv.at[step, 2])
        wait_bytes(of_x_core(step, 1, x_far), x_recv.at[step, 3])

    table_copies = [
        pltpu.make_async_copy(t_made.at[pl.ds(i, 1)], to, t_sem.at[i])
        for i, to in enumerate((col_at, which_at, goes_on_at, last_at))
    ]

    def make_table():
        listed = (TILES, TILES)
        down = lax.broadcasted_iota(jnp.int32, listed, 0)
        along = lax.broadcasted_iota(jnp.int32, listed, 1)
        row_along = jnp.broadcast_to(t_rows[...], listed)
        col_along = jnp.broadcast_to(t_cols[...] + HB, listed)
        row_down = jnp.sum(jnp.where(down == along, row_along, 0), axis=1, keepdims=True)
        col_down = jnp.sum(jnp.where(down == along, col_along, 0), axis=1, keepdims=True)
        same_before = (row_along == row_down) & (along < down) & (along >= BLOCKS)
        before = same_before | ((row_along < row_down) & (along >= BLOCKS))
        place = jnp.sum(jnp.where(before, 1, 0), axis=1, keepdims=True)
        goes_on = jnp.minimum(jnp.sum(jnp.where(same_before, 1, 0), axis=1, keepdims=True), 1)
        here = (place == along) & (down >= BLOCKS)

        def in_order(values):
            return jnp.sum(jnp.where(here, values, 0), axis=0, keepdims=True)

        is_extra = down >= BLOCKS
        up_to = jnp.sum(jnp.where(is_extra & (row_down <= along), 1, 0), axis=0, keepdims=True)
        below = jnp.sum(jnp.where(is_extra & (row_down < along), 1, 0), axis=0, keepdims=True)
        t_made[0:1] = in_order(col_down)
        t_made[1:2] = in_order(down - BLOCKS)
        t_made[2:3] = in_order(goes_on)
        t_made[3:4] = jnp.where(up_to > below, up_to - 1, EXTRA)
        for made in table_copies:
            made.start()

    def times_tile(rows, tile):
        return lax.dot_general(rows, tile, (((1,), (1,)), ((), ())), preferred_element_type=F32)

    def apply_diagonal(ext):
        def body(i, carry):
            for u in range(UNROLL):
                b = i * UNROLL + u
                acc[b] = times_tile(ext[b + HB], diag[b])
            return carry

        lax.fori_loop(0, BLOCKS // UNROLL, body, 0)

    def apply_extra(ext):
        def multiply(i, carry):
            for u in range(UNROLL):
                m = i * UNROLL + u
                seg[m] = times_tile(ext[col_at[0, m]], extra[which_at[0, m]])
            return carry

        lax.fori_loop(0, EXTRA // UNROLL, multiply, 0)

        def add_up(i, run):
            for u in range(UNROLL):
                m = i * UNROLL + u
                run = seg[m] + goes_on_at[0, m].astype(F32) * run
                seg[m] = run
            return run

        lax.fori_loop(0, EXTRA // UNROLL, add_up, jnp.zeros((NORB_DEV, TILE), F32))

    lanes = lax.broadcasted_iota(jnp.int32, (1, TILE), 1)

    def filtered_first(b):
        total = acc[b] + seg[last_at[0, b]]
        source = e0[b + HB].astype(F32)
        value = (total - coef[0, 0:1] * source) * coef[1, 0:1]
        e1[b + HB] = jnp.where(lanes < counts[b], value, 0.0).astype(BF16)

    def filtered_second(b):
        total = acc[b] + seg[last_at[0, b]]
        source = e0[b + HB].astype(F32)
        first = e1[b + HB].astype(F32)
        value = (total - coef[0, 0:1] * first) * coef[2, 0:1] - coef[3, 0:1] * source
        return jnp.where(lanes < counts[b], value, 0.0).astype(BF16)

    loads[0].wait()
    loads[5].wait()
    make_table()
    loads[3].wait()
    apply_diagonal(e0)
    loads[4].wait()
    for made in table_copies:
        made.wait()
    loads[6].wait()
    wait_edges(e0, 0)
    apply_extra(e0)
    for b in (0, 1, BLOCKS - 2, BLOCKS - 1):
        filtered_first(b)
    send_edges(e1, 1)

    def inner_first(i, carry):
        for u in range(4):
            filtered_first(HB + 4 * i + u)
        return carry

    lax.fori_loop(0, (BLOCKS - 2 * HB) // 4, inner_first, 0)
    apply_diagonal(e1)
    stage_one(0)
    wait_edges(e1, 1)
    apply_extra(e1)
    stage_one(1)

    def destination(i):
        return lax.rem(x + i // NZ, NX) * NZ + lax.rem(z + lax.rem(i, NZ), NZ)

    def f_one(i, carry):
        there = destination(i)
        f2[there, :, :TILE] = filtered_second(2 * there)
        f2[there, :, TILE:] = filtered_second(2 * there + 1)

        @pl.when(i > 0)
        def _():
            send(f2.at[there], fb.at[core, chip, :, pl.ds(0, PAIR)], f_send, f_recv.at[x], (s, there * 2 + core))

        @pl.when(i == 0)
        def _():
            pltpu.make_async_copy(f2.at[there], fb.at[core, chip, :, pl.ds(0, PAIR)], f_recv.at[x]).start()

        return carry

    lax.fori_loop(0, CHIPS, f_one, 0)

    def turn(at_core, at_x, first_row):
        for group in range(2):
            block = fb[at_core, pl.ds(at_x * NZ + 4 * group, 4), :, first_row:first_row + TILE]
            k = at_core * (CHIPS * NORB_DEV) + (at_x * 2 + group) * TILE
            ft[first_row:first_row + TILE, aligned(k // TILE, TILE)] = block.reshape(TILE, TILE).T

    def pass_on(at_x):
        at = pl.ds(at_x * NZ, NZ)
        got = fb.at[core, at, :, pl.ds(0, PAIR)]
        wait_bytes(got, f_recv.at[at_x])
        for to in (o, partner):
            send(fb.at[core, at, :, pl.ds(0, TILE)], fb.at[core, at, :, pl.ds(PAIR, TILE)],
                 g_send, g_recv.at[at_x, 1], (s_up, to))
            send(fb.at[core, at, :, pl.ds(TILE, TILE)], fb.at[core, at, :, pl.ds(PAIR + TILE, TILE)],
                 g_send, g_recv.at[at_x, 2], (s_down, to))
        send(got, got, g_send, g_recv.at[at_x, 0], (s, partner))
        turn(core, at_x, 0)
        turn(core, at_x, TILE)

    def take(at_x):
        at = pl.ds(at_x * NZ, NZ)
        wait_bytes(fb.at[1 - core, at, :, pl.ds(0, PAIR)], g_recv.at[at_x, 0])
        turn(1 - core, at_x, 0)
        turn(1 - core, at_x, TILE)
        for side in range(2):
            wait_bytes(fb.at[:, at, :, pl.ds(PAIR + side * TILE, TILE)], g_recv.at[at_x, 1 + side])
            turn(0, at_x, PAIR + side * TILE)
            turn(1, at_x, PAIR + side * TILE)

    def back_x(i):
        return lax.rem(x + NX - i, NX)

    stage_one(2)
    stage_one(3)
    stage_two(0)
    stage_two(1)
    pass_on(back_x(0))
    stage_three(0)
    stage_two(2)
    pass_on(back_x(1))
    stage_three(1)
    stage_two(3)
    pass_on(back_x(2))
    stage_three(2)
    pass_on(back_x(3))
    for i in range(NX):
        take(back_x(i))
    stage_three(3)

    def rotate(step, carry):
        slot = rb[step].reshape(2 * CHIPS * NORB_DEV, TILE)
        made = jnp.dot(ft[...], slot, preferred_element_type=F32)
        ob[step] = made.T.astype(BF16)
        first = column_group(core, half, step, z) * 4
        own = pl.ds(pl.multiple_of(chip * PAIR, PAIR), PAIR)
        low = pl.ds(pl.multiple_of(chip * PAIR, TILE), TILE)
        high = pl.ds(pl.multiple_of(chip * PAIR + TILE, TILE), TILE)
        for i in range(4):
            rows = pl.ds(i * NORB_DEV, NORB_DEV)
            owner = first + i
            send(ob.at[step, rows, pl.ds(PAIR, TILE)], ov.at[:, low], o_send, o_recv, (s_down, owner))
            send(ob.at[step, rows, pl.ds(PAIR + TILE, TILE)], ov.at[:, high], o_send, o_recv, (s_up, owner))
            piece = ob.at[step, rows, pl.ds(0, PAIR)]

            @pl.when(owner == o)
            def _():
                pltpu.make_async_copy(piece, ov.at[:, own], o_recv).start()

            @pl.when(owner != o)
            def _():
                send(piece, ov.at[:, own], o_send, o_recv, (s, owner))

        return carry

    lax.fori_loop(0, STEPS, rotate, 0)

    wait_bytes(ov, o_recv)
    store = pltpu.make_async_copy(ov, out_hbm, out_sem)
    store.start()
    for which, ext in ((0, e0), (1, e1)):
        @pl.when(not_last)
        def _():
            wait_bytes(ext.at[low_edge], h_send.at[which, 0])

        @pl.when(not_first)
        def _():
            wait_bytes(ext.at[high_edge], h_send.at[which, 1])

    wait_bytes(rb.at[0, :, pl.ds(0, 30)], z_send)
    wait_bytes(rb.at[pl.ds(0, 3)], x_send)
    wait_bytes(f2.at[pl.ds(0, CHIPS - 1)], f_send)
    wait_bytes(fb.at[:, :, :, pl.ds(0, PAIR + TILE)], g_send)
    mine_too = (x // 2 == core) & (lax.rem(z // 2, 2) == half)

    @pl.when(mine_too)
    def _():
        wait_bytes(f2.at[pl.ds(0, CHIPS - 1)], o_send)

    @pl.when(jnp.logical_not(mine_too))
    def _():
        wait_bytes(f2, o_send)

    store.wait()


def local(orbitals_t, tiles, tile_rows, tile_cols, row_counts, bounds, rotation):
    dma = pltpu.SemaphoreType.DMA
    ext = pltpu.VMEM((BLOCKS + 2 * HB, NORB_DEV, TILE), BF16)
    anywhere = pl.BlockSpec(memory_space=pl.ANY)
    return pl.pallas_call(
        kernel,
        out_shape=jax.ShapeDtypeStruct(orbitals_t.shape, BF16),
        in_specs=[anywhere] * 7,
        out_specs=anywhere,
        scratch_shapes=[
            *[pltpu.VMEM((1, TILES), jnp.int32)] * 2,
            pltpu.VMEM((8, TILES), jnp.int32),
            *[pltpu.SMEM((1, TILES), jnp.int32)] * 4,
            pltpu.SMEM((BLOCKS,), jnp.int32),
            pltpu.SMEM((3,), F32),
            ext, ext,
            pltpu.VMEM((BLOCKS, TILE, TILE), BF16),
            pltpu.VMEM((EXTRA, TILE, TILE), BF16),
            pltpu.VMEM((BLOCKS, NORB_DEV, TILE), F32),
            pltpu.VMEM((EXTRA + 1, NORB_DEV, TILE), F32),
            pltpu.VMEM((4, 8, TILE), F32),
            pltpu.VMEM((CHIPS, NORB_DEV, PAIR), BF16),
            pltpu.VMEM((NORB_DEV, N_ORB * NORB_DEV), BF16),
            pltpu.VMEM((STEPS, 2, CHIPS, NORB_DEV, TILE), BF16),
            pltpu.VMEM((2, CHIPS, NORB_DEV, 2 * PAIR), BF16),
            pltpu.VMEM((2 * PAIR, N_ORB * NORB_DEV), BF16),
            pltpu.VMEM((STEPS, TILE, 2 * PAIR), BF16),
            pltpu.VMEM((NORB_DEV, ROWS_DEV), BF16),
            dma((8,)), dma((4,)), dma((2, 2)), dma((2, 2)), dma, dma((STEPS,)), dma, dma((STEPS, 4)),
            dma, dma((NX,)), dma, dma((NX, 3)), dma, dma, dma,
        ],
        compiler_params=pltpu.CompilerParams(
            collective_id=0, has_side_effects=True, vmem_limit_bytes=40 << 20
        ),
    )(
        *(pltpu.with_memory_space_constraint(v, pltpu.HBM) for v in (
            tile_rows.reshape(1, TILES), tile_cols.reshape(1, TILES), row_counts, bounds, orbitals_t, tiles, rotation,
        ))
    )


def solution(mesh):
    return jax.shard_map(
        local,
        mesh=mesh,
        in_specs=(
            P("orb", "slab"),
            P("slab", None, None),
            P("slab"),
            P("slab"),
            P("slab"),
            P(),
            P("orb", None),
        ),
        out_specs=P("orb", "slab"),
        check_vma=False,
    )
```

```python
import jax
import jax.numpy as jnp
from jax import lax
from jax.experimental import pallas as pl
from jax.experimental.pallas import tpu as pltpu
from jax.sharding import PartitionSpec as P

HB = 2
NX, NZ = 4, 8
CHIPS = NX * NZ
N_SLAB = 8
N_ORB = 2 * CHIPS
NORB_DEV = 32
TILE = 128
PAIR = 2 * TILE
BLOCKS = 64
EXTRA = 48
TILES = BLOCKS + EXTRA
ROWS_DEV = BLOCKS * TILE
STEPS = 4
UNROLL = 8
MESH = pl.DeviceIdType.MESH
BF16, F32 = jnp.bfloat16, jnp.float32


def column_group(core, half, step, z):
    owner_x = 2 * core + lax.rem(step + z, 2)
    z_pair = half + 2 * lax.rem(step // 2 + z // 2, 2)
    return owner_x * 4 + z_pair


def aligned(index, size):
    return pl.ds(pl.multiple_of(index * size, size), size)


def kernel(
    rows_hbm, cols_hbm, counts_hbm, bounds_hbm, orb_hbm, tiles_hbm, r_hbm, out,
    t_rows, t_cols, t_made, col_at, which_at, goes_on_at, last_at, counts, bounds, e0, e1, diag, extra, acc, seg, coef, f2, rv, rb, fb, ft, ob,
    in_sem, t_sem, h_send, h_recv, z_send, z_recv, x_send, x_recv, y_send, y_recv,
    f_send, f_recv, g_send, g_recv, o_send, o_recv,
):
    s, o = lax.axis_index("slab"), lax.axis_index("orb")
    core, chip = lax.rem(o, 2), o // 2
    z, x = lax.rem(chip, NZ), chip // NZ
    half = lax.rem(s, 2)
    partner = o + 1 - 2 * core
    x_up, x_down = lax.rem(x + 1, NX), lax.rem(x + NX - 1, NX)
    x_far = lax.rem(x + 2, NX)
    turn_of = lax.rem(s // 2, 2)
    s_two_up, s_two_down = lax.rem(s + 2, N_SLAB), lax.rem(s + N_SLAB - 2, N_SLAB)
    s_up, s_down = lax.rem(s + 1, N_SLAB), lax.rem(s + N_SLAB - 1, N_SLAB)
    not_first, not_last = s > 0, s < N_SLAB - 1

    loads = [
        pltpu.make_async_copy(rows_hbm, t_rows, in_sem.at[0]),
        pltpu.make_async_copy(bounds_hbm, bounds, in_sem.at[4]),
        pltpu.make_async_copy(r_hbm, rv, in_sem.at[1]),
        pltpu.make_async_copy(tiles_hbm.at[pl.ds(0, BLOCKS)], diag, in_sem.at[2]),
        pltpu.make_async_copy(tiles_hbm.at[pl.ds(BLOCKS, EXTRA)], extra, in_sem.at[3]),
        pltpu.make_async_copy(cols_hbm, t_cols, in_sem.at[6]),
        pltpu.make_async_copy(counts_hbm, counts, in_sem.at[7]),
    ]
    for load in loads:
        load.start()

    def load_block(b, carry):
        pltpu.make_async_copy(orb_hbm.at[:, aligned(b, TILE)], e0.at[HB + b], in_sem.at[5]).start()
        return carry

    lax.fori_loop(0, BLOCKS, load_block, 0)

    def wait_bytes(ref, sem):
        pltpu.make_async_copy(ref, ref, sem).wait()

    barrier = pltpu.get_barrier_semaphore()

    same_parity = lax.rem(z // 2, 2) == half

    def signal(to):
        pl.semaphore_signal(barrier, inc=1, device_id=to, device_id_type=MESH)

    def greet_chip(i, carry):
        signal((s, lax.rem(chip + i, CHIPS) * 2 + core))
        return carry

    def greet_column(i, carry):
        signal((s, (x * NZ + i) * 2 + 1 - core))
        return carry

    def greet_other(i, carry):
        signal((s, lax.rem(chip + i, CHIPS) * 2 + 1 - core))
        return carry

    def greet_near(i, carry):
        for near in (s_up, s_down):
            signal((near, lax.rem(chip + i, CHIPS) * 2 + x // 2))
        return carry

    for near in (s_up, s_down, s_two_up, s_two_down):
        signal((near, o))
    lax.fori_loop(1, CHIPS, greet_chip, 0)
    lax.fori_loop(0, NZ, greet_column, 0)
    lax.fori_loop(0, jnp.where(same_parity & (core != x // 2), CHIPS, 0), greet_other, 0)
    lax.fori_loop(0, jnp.where(same_parity, 0, CHIPS), greet_near, 0)

    loads[1].wait()
    lower = jnp.full((8, TILE), bounds[0]) - 3.0
    cutoff = jnp.full((8, TILE), bounds[1]) - 0.5
    upper = jnp.full((8, TILE), bounds[2]) + 3.0
    half_width = (upper - cutoff) / 2.0
    center = (upper + cutoff) / 2.0
    sigma_one = half_width / (lower - center)
    sigma_two = 1.0 / (2.0 / sigma_one - sigma_one)
    coef[0] = center
    coef[1] = sigma_one / half_width
    coef[2] = 2.0 * sigma_two / half_width
    coef[3] = sigma_one * sigma_two

    for ext in (e0, e1):
        @pl.when(s == 0)
        def _():
            ext[:HB] = jnp.zeros((HB, NORB_DEV, TILE), BF16)

        @pl.when(s == N_SLAB - 1)
        def _():
            ext[HB + BLOCKS:] = jnp.zeros((HB, NORB_DEV, TILE), BF16)

    seg[EXTRA] = jnp.zeros((NORB_DEV, TILE), F32)

    loads[2].wait()
    wait_bytes(e0.at[pl.ds(HB, BLOCKS)], in_sem.at[5])
    pl.semaphore_wait(barrier, 4 + (CHIPS - 1) + NZ + 8 + 32)

    def send(src, dst, send_sem, recv_sem, to):
        pltpu.make_async_remote_copy(
            src_ref=src, dst_ref=dst, send_sem=send_sem, recv_sem=recv_sem,
            device_id=to, device_id_type=MESH,
        ).start()

    low_edge, high_edge = pl.ds(0, HB), pl.ds(HB + BLOCKS, HB)

    def send_edges(ext, which):
        @pl.when(not_last)
        def _():
            send(ext.at[pl.ds(BLOCKS, HB)], ext.at[low_edge],
                 h_send.at[which, 0], h_recv.at[which, 0], (s_up, o))

        @pl.when(not_first)
        def _():
            send(ext.at[pl.ds(HB, HB)], ext.at[high_edge],
                 h_send.at[which, 1], h_recv.at[which, 1], (s_down, o))

    def wait_edges(ext, which):
        @pl.when(not_first)
        def _():
            wait_bytes(ext.at[low_edge], h_recv.at[which, 0])

        @pl.when(not_last)
        def _():
            wait_bytes(ext.at[high_edge], h_recv.at[which, 1])

    send_edges(e0, 0)

    def rotation_columns(to_core, step, to_z):
        return rv.at[:, aligned(column_group(to_core, half, step, to_z), TILE)]

    def z_step(i, carry):
        step = jnp.where(i == 0, turn_of, i + 1)
        pltpu.make_async_copy(
            rotation_columns(core, step, z), rb.at[step, core, chip], z_recv.at[step]
        ).start()

        def one(j, inner):
            there = lax.rem(z * 2 + core + j, 2 * NZ)
            send(
                rotation_columns(lax.rem(there, 2), step, there // 2),
                rb.at[step, core, chip], z_send, z_recv.at[step], (s, x * 2 * NZ + there),
            )
            return inner

        lax.fori_loop(1, 2 * NZ, one, 0)
        return carry

    lax.fori_loop(0, STEPS - 1, z_step, 0)

    def of_x(step, at_x):
        return rb.at[step, :, pl.ds(at_x * NZ, NZ)]

    def of_x_core(step, at_core, at_x):
        return rb.at[step, at_core, pl.ds(at_x * NZ, NZ)]

    def orb_at(at_x):
        return (at_x * NZ + z) * 2 + core

    def to_slabs(step, at_x):
        low, high = of_x_core(step, 0, at_x), of_x_core(step, 1, at_x)
        send(low, low, y_send, y_recv, (s_two_up, o))
        send(high, high, y_send, y_recv, (s_two_down, o))

    def stage_one(step):
        mine = of_x(step, x)
        wait_bytes(mine, z_recv.at[step])
        send(mine, mine, x_send, x_recv.at[step, 0], (s, orb_at(x_up)))
        send(mine, mine, x_send, x_recv.at[step, 1], (s, orb_at(x_down)))

    def stage_two(step):
        wait_bytes(of_x(step, x_down), x_recv.at[step, 0])
        relayed = of_x_core(step, 0, x_down)
        send(relayed, relayed, x_send, x_recv.at[step, 2], (s, orb_at(x_up)))
        wait_bytes(of_x(step, x_up), x_recv.at[step, 1])
        relayed = of_x_core(step, 1, x_up)
        send(relayed, relayed, x_send, x_recv.at[step, 3], (s, orb_at(x_down)))

    def stage_three(step):
        wait_bytes(of_x_core(step, 0, x_far), x_recv.at[step, 2])
        wait_bytes(of_x_core(step, 1, x_far), x_recv.at[step, 3])

    table_copies = [
        pltpu.make_async_copy(t_made.at[pl.ds(i, 1)], to, t_sem.at[i])
        for i, to in enumerate((col_at, which_at, goes_on_at, last_at))
    ]

    def make_table():
        listed = (TILES, TILES)
        down = lax.broadcasted_iota(jnp.int32, listed, 0)
        along = lax.broadcasted_iota(jnp.int32, listed, 1)
        row_along = jnp.broadcast_to(t_rows[...], listed)
        col_along = jnp.broadcast_to(t_cols[...] + HB, listed)
        row_down = jnp.sum(jnp.where(down == along, row_along, 0), axis=1, keepdims=True)
        col_down = jnp.sum(jnp.where(down == along, col_along, 0), axis=1, keepdims=True)
        same_before = (row_along == row_down) & (along < down) & (along >= BLOCKS)
        before = same_before | ((row_along < row_down) & (along >= BLOCKS))
        place = jnp.sum(jnp.where(before, 1, 0), axis=1, keepdims=True)
        goes_on = jnp.minimum(jnp.sum(jnp.where(same_before, 1, 0), axis=1, keepdims=True), 1)
        here = (place == along) & (down >= BLOCKS)

        def in_order(values):
            return jnp.sum(jnp.where(here, values, 0), axis=0, keepdims=True)

        is_extra = down >= BLOCKS
        up_to = jnp.sum(jnp.where(is_extra & (row_down <= along), 1, 0), axis=0, keepdims=True)
        below = jnp.sum(jnp.where(is_extra & (row_down < along), 1, 0), axis=0, keepdims=True)
        t_made[0:1] = in_order(col_down)
        t_made[1:2] = in_order(down - BLOCKS)
        t_made[2:3] = in_order(goes_on)
        t_made[3:4] = jnp.where(up_to > below, up_to - 1, EXTRA)
        for made in table_copies:
            made.start()

    def times_tile(rows, tile):
        return lax.dot_general(rows, tile, (((1,), (1,)), ((), ())), preferred_element_type=F32)

    def apply_diagonal(ext):
        def body(i, carry):
            for u in range(UNROLL):
                b = i * UNROLL + u
                acc[b] = times_tile(ext[b + HB], diag[b])
            return carry

        lax.fori_loop(0, BLOCKS // UNROLL, body, 0)

    def apply_extra(ext):
        def multiply(i, carry):
            for u in range(UNROLL):
                m = i * UNROLL + u
                seg[m] = times_tile(ext[col_at[0, m]], extra[which_at[0, m]])
            return carry

        lax.fori_loop(0, EXTRA // UNROLL, multiply, 0)

        def add_up(i, run):
            for u in range(UNROLL):
                m = i * UNROLL + u
                run = seg[m] + goes_on_at[0, m].astype(F32) * run
                seg[m] = run
            return run

        lax.fori_loop(0, EXTRA // UNROLL, add_up, jnp.zeros((NORB_DEV, TILE), F32))

    lanes = lax.broadcasted_iota(jnp.int32, (1, TILE), 1)

    def filtered_first(b):
        total = acc[b] + seg[last_at[0, b]]
        source = e0[b + HB].astype(F32)
        value = (total - coef[0, 0:1] * source) * coef[1, 0:1]
        e1[b + HB] = jnp.where(lanes < counts[b], value, 0.0).astype(BF16)

    def filtered_second(b):
        total = acc[b] + seg[last_at[0, b]]
        source = e0[b + HB].astype(F32)
        first = e1[b + HB].astype(F32)
        value = (total - coef[0, 0:1] * first) * coef[2, 0:1] - coef[3, 0:1] * source
        return jnp.where(lanes < counts[b], value, 0.0).astype(BF16)

    loads[0].wait()
    loads[5].wait()
    make_table()
    loads[3].wait()
    apply_diagonal(e0)
    loads[4].wait()
    for made in table_copies:
        made.wait()
    loads[6].wait()
    wait_edges(e0, 0)
    apply_extra(e0)
    for b in (0, 1, BLOCKS - 2, BLOCKS - 1):
        filtered_first(b)
    send_edges(e1, 1)

    def inner_first(i, carry):
        for u in range(4):
            filtered_first(HB + 4 * i + u)
        return carry

    lax.fori_loop(0, (BLOCKS - 2 * HB) // 4, inner_first, 0)
    apply_diagonal(e1)
    stage_one(turn_of)
    to_slabs(turn_of, x)
    wait_edges(e1, 1)
    apply_extra(e1)
    stage_one(2)

    def destination(i):
        return lax.rem(x + i // NZ, NX) * NZ + lax.rem(z + lax.rem(i, NZ), NZ)

    def f_one(i, carry):
        there = destination(i)
        f2[there, :, :TILE] = filtered_second(2 * there)
        f2[there, :, TILE:] = filtered_second(2 * there + 1)

        @pl.when(i > 0)
        def _():
            send(f2.at[there], fb.at[core, chip, :, pl.ds(0, PAIR)], f_send, f_recv.at[x], (s, there * 2 + core))

        @pl.when(i == 0)
        def _():
            pltpu.make_async_copy(f2.at[there], fb.at[core, chip, :, pl.ds(0, PAIR)], f_recv.at[x]).start()

        return carry

    lax.fori_loop(0, CHIPS, f_one, 0)

    def turn(at_core, at_x, first_row):
        for group in range(2):
            block = fb[at_core, pl.ds(at_x * NZ + 4 * group, 4), :, first_row:first_row + TILE]
            k = at_core * (CHIPS * NORB_DEV) + (at_x * 2 + group) * TILE
            ft[first_row:first_row + TILE, aligned(k // TILE, TILE)] = block.reshape(TILE, TILE).T

    def pass_on(at_x):
        at = pl.ds(at_x * NZ, NZ)
        got = fb.at[core, at, :, pl.ds(0, PAIR)]
        wait_bytes(got, f_recv.at[at_x])
        send(fb.at[core, at, :, pl.ds(0, TILE)], fb.at[core, at, :, pl.ds(PAIR, TILE)],
             g_send, g_recv.at[at_x, 1], (s_up, o))
        send(fb.at[core, at, :, pl.ds(TILE, TILE)], fb.at[core, at, :, pl.ds(PAIR + TILE, TILE)],
             g_send, g_recv.at[at_x, 2], (s_down, o))
        send(got, got, g_send, g_recv.at[at_x, 0], (s, partner))
        turn(core, at_x, 0)
        turn(core, at_x, TILE)

    def relay(at_x):
        at = pl.ds(at_x * NZ, NZ)
        for side in range(2):
            wait_bytes(fb.at[core, at, :, pl.ds(PAIR + side * TILE, TILE)], g_recv.at[at_x, 1 + side])
        got = fb.at[core, at, :, pl.ds(PAIR, PAIR)]
        send(got, got, g_send, g_recv.at[at_x, 3], (s, partner))
        turn(core, at_x, PAIR)
        turn(core, at_x, PAIR + TILE)

    def take(at_x):
        at = pl.ds(at_x * NZ, NZ)
        for part, which in ((0, 0), (1, 3)):
            wait_bytes(fb.at[1 - core, at, :, pl.ds(part * PAIR, PAIR)], g_recv.at[at_x, which])
            turn(1 - core, at_x, part * PAIR)
            turn(1 - core, at_x, part * PAIR + TILE)

    def back_x(i):
        return lax.rem(x + NX - i, NX)

    stage_two(turn_of)
    to_slabs(turn_of, x_down)
    to_slabs(turn_of, x_up)
    stage_one(3)
    stage_two(2)
    stage_three(turn_of)
    to_slabs(turn_of, x_far)
    pass_on(back_x(0))
    pass_on(back_x(1))
    relay(back_x(0))
    stage_two(3)
    pass_on(back_x(2))
    relay(back_x(1))
    stage_three(2)
    pass_on(back_x(3))
    relay(back_x(2))
    take(back_x(0))
    take(back_x(1))
    relay(back_x(3))
    take(back_x(2))
    take(back_x(3))
    stage_three(3)
    wait_bytes(rb.at[1 - turn_of], y_recv)

    def rotate(step, carry):
        slot = rb[step].reshape(2 * CHIPS * NORB_DEV, TILE)
        made = jnp.dot(ft[...], slot, preferred_element_type=F32)
        ob[step] = made.T.astype(BF16)
        first = column_group(core, half, step, z) * 4
        own = pl.ds(pl.multiple_of(chip * PAIR, PAIR), PAIR)
        low = pl.ds(pl.multiple_of(chip * PAIR, TILE), TILE)
        high = pl.ds(pl.multiple_of(chip * PAIR + TILE, TILE), TILE)
        for i in range(4):
            rows = pl.ds(i * NORB_DEV, NORB_DEV)
            owner = first + i
            send(ob.at[step, rows, pl.ds(PAIR, TILE)], out.at[:, low], o_send, o_recv, (s_down, owner))
            send(ob.at[step, rows, pl.ds(PAIR + TILE, TILE)], out.at[:, high], o_send, o_recv, (s_up, owner))
            piece = ob.at[step, rows, pl.ds(0, PAIR)]

            @pl.when(owner == o)
            def _():
                pltpu.make_async_copy(piece, out.at[:, own], o_recv).start()

            @pl.when(owner != o)
            def _():
                send(piece, out.at[:, own], o_send, o_recv, (s, owner))

        return carry

    lax.fori_loop(0, STEPS, rotate, 0)

    for which, ext in ((0, e0), (1, e1)):
        @pl.when(not_last)
        def _():
            wait_bytes(ext.at[low_edge], h_send.at[which, 0])

        @pl.when(not_first)
        def _():
            wait_bytes(ext.at[high_edge], h_send.at[which, 1])

    wait_bytes(rb.at[pl.ds(0, 3), 0, pl.ds(0, 15)], z_send)
    wait_bytes(rb.at[pl.ds(0, 3), :, pl.ds(0, 24)], x_send)
    wait_bytes(rb.at[0], y_send)
    wait_bytes(f2.at[pl.ds(0, CHIPS - 1)], f_send)
    wait_bytes(fb.at[:, :, :, pl.ds(0, PAIR + TILE)], g_send)
    mine_too = (x // 2 == core) & (lax.rem(z // 2, 2) == half)

    @pl.when(mine_too)
    def _():
        wait_bytes(f2.at[pl.ds(0, CHIPS - 1)], o_send)

    @pl.when(jnp.logical_not(mine_too))
    def _():
        wait_bytes(f2, o_send)

    wait_bytes(out, o_recv)


def local(orbitals_t, tiles, tile_rows, tile_cols, row_counts, bounds, rotation):
    dma = pltpu.SemaphoreType.DMA
    ext = pltpu.VMEM((BLOCKS + 2 * HB, NORB_DEV, TILE), BF16)
    anywhere = pl.BlockSpec(memory_space=pl.ANY)
    return pl.pallas_call(
        kernel,
        out_shape=jax.ShapeDtypeStruct(orbitals_t.shape, BF16),
        in_specs=[anywhere] * 7,
        out_specs=anywhere,
        scratch_shapes=[
            *[pltpu.VMEM((1, TILES), jnp.int32)] * 2,
            pltpu.VMEM((8, TILES), jnp.int32),
            *[pltpu.SMEM((1, TILES), jnp.int32)] * 4,
            pltpu.SMEM((BLOCKS,), jnp.int32),
            pltpu.SMEM((3,), F32),
            ext, ext,
            pltpu.VMEM((BLOCKS, TILE, TILE), BF16),
            pltpu.VMEM((EXTRA, TILE, TILE), BF16),
            pltpu.VMEM((BLOCKS, NORB_DEV, TILE), F32),
            pltpu.VMEM((EXTRA + 1, NORB_DEV, TILE), F32),
            pltpu.VMEM((4, 8, TILE), F32),
            pltpu.VMEM((CHIPS, NORB_DEV, PAIR), BF16),
            pltpu.VMEM((NORB_DEV, N_ORB * NORB_DEV), BF16),
            pltpu.VMEM((STEPS, 2, CHIPS, NORB_DEV, TILE), BF16),
            pltpu.VMEM((2, CHIPS, NORB_DEV, 2 * PAIR), BF16),
            pltpu.VMEM((2 * PAIR, N_ORB * NORB_DEV), BF16),
            pltpu.VMEM((STEPS, TILE, 2 * PAIR), BF16),
            dma((8,)), dma((4,)), dma((2, 2)), dma((2, 2)), dma, dma((STEPS,)), dma, dma((STEPS, 4)), dma, dma,
            dma, dma((NX,)), dma, dma((NX, 4)), dma, dma,
        ],
        compiler_params=pltpu.CompilerParams(
            collective_id=0, has_side_effects=True, vmem_limit_bytes=40 << 20
        ),
    )(
        *(pltpu.with_memory_space_constraint(v, pltpu.HBM) for v in (
            tile_rows.reshape(1, TILES), tile_cols.reshape(1, TILES), row_counts, bounds, orbitals_t, tiles, rotation,
        ))
    )


def solution(mesh):
    return jax.shard_map(
        local,
        mesh=mesh,
        in_specs=(
            P("orb", "slab"),
            P("slab", None, None),
            P("slab"),
            P("slab"),
            P("slab"),
            P(),
            P("orb", None),
        ),
        out_specs=P("orb", "slab"),
        check_vma=False,
    )
```

```python
import jax
import jax.numpy as jnp
from jax import lax
from jax.experimental import pallas as pl
from jax.experimental.pallas import tpu as pltpu
from jax.sharding import PartitionSpec as P

HB = 2
NX, NZ = 4, 8
CHIPS = NX * NZ
N_SLAB = 8
N_ORB = 2 * CHIPS
NORB_DEV = 32
TILE = 128
PAIR = 2 * TILE
BLOCKS = 64
EXTRA = 48
TILES = BLOCKS + EXTRA
ROWS_DEV = BLOCKS * TILE
STEPS = 4
UNROLL = 8
MESH = pl.DeviceIdType.MESH
BF16, F32 = jnp.bfloat16, jnp.float32


def column_group(core, half, step, z):
    owner_x = 2 * core + lax.rem(step + z, 2)
    z_pair = half + 2 * lax.rem(step // 2 + z // 2, 2)
    return owner_x * 4 + z_pair


def aligned(index, size):
    return pl.ds(pl.multiple_of(index * size, size), size)


def kernel(
    rows_hbm, cols_hbm, counts_hbm, bounds_hbm, orb_hbm, tiles_hbm, r_hbm, out,
    t_rows, t_cols, t_made, col_at, which_at, goes_on_at, last_at, counts, bounds, e0, e1, diag, extra, acc, seg, coef, f2, rv, rb, fb, ft, ob,
    in_sem, t_sem, h_send, h_recv, z_send, z_recv, x_send, x_recv, y_send, y_recv,
    f_send, f_recv, g_send, g_recv, o_send, o_recv,
):
    s, o = lax.axis_index("slab"), lax.axis_index("orb")
    core, chip = lax.rem(o, 2), o // 2
    z, x = lax.rem(chip, NZ), chip // NZ
    half = lax.rem(s, 2)
    partner = o + 1 - 2 * core
    x_up, x_down = lax.rem(x + 1, NX), lax.rem(x + NX - 1, NX)
    x_far = lax.rem(x + 2, NX)
    turn_of = lax.rem(s // 2, 2)
    s_two_up, s_two_down = lax.rem(s + 2, N_SLAB), lax.rem(s + N_SLAB - 2, N_SLAB)
    s_up, s_down = lax.rem(s + 1, N_SLAB), lax.rem(s + N_SLAB - 1, N_SLAB)
    not_first, not_last = s > 0, s < N_SLAB - 1

    loads = [
        pltpu.make_async_copy(rows_hbm, t_rows, in_sem.at[0]),
        pltpu.make_async_copy(bounds_hbm, bounds, in_sem.at[4]),
        pltpu.make_async_copy(r_hbm, rv, in_sem.at[1]),
        pltpu.make_async_copy(tiles_hbm.at[pl.ds(0, BLOCKS)], diag, in_sem.at[2]),
        pltpu.make_async_copy(tiles_hbm.at[pl.ds(BLOCKS, EXTRA)], extra, in_sem.at[3]),
        pltpu.make_async_copy(cols_hbm, t_cols, in_sem.at[6]),
        pltpu.make_async_copy(counts_hbm, counts, in_sem.at[7]),
    ]
    for load in loads:
        load.start()

    def load_block(b, carry):
        pltpu.make_async_copy(orb_hbm.at[:, aligned(b, TILE)], e0.at[HB + b], in_sem.at[5]).start()
        return carry

    lax.fori_loop(0, BLOCKS, load_block, 0)

    def wait_bytes(ref, sem):
        pltpu.make_async_copy(ref, ref, sem).wait()

    barrier = pltpu.get_barrier_semaphore()

    same_parity = lax.rem(z // 2, 2) == half

    def signal(to):
        pl.semaphore_signal(barrier, inc=1, device_id=to, device_id_type=MESH)

    def greet_chip(i, carry):
        signal((s, lax.rem(chip + i, CHIPS) * 2 + core))
        return carry

    def greet_column(i, carry):
        signal((s, (x * NZ + i) * 2 + 1 - core))
        return carry

    def greet_other(i, carry):
        signal((s, lax.rem(chip + i, CHIPS) * 2 + 1 - core))
        return carry

    def greet_near(i, carry):
        for near in (s_up, s_down):
            signal((near, lax.rem(chip + i, CHIPS) * 2 + x // 2))
        return carry

    for near in (s_up, s_down, s_two_up, s_two_down):
        signal((near, o))
    lax.fori_loop(1, CHIPS, greet_chip, 0)
    lax.fori_loop(0, NZ, greet_column, 0)
    lax.fori_loop(0, jnp.where(same_parity & (core != x // 2), CHIPS, 0), greet_other, 0)
    lax.fori_loop(0, jnp.where(same_parity, 0, CHIPS), greet_near, 0)

    loads[1].wait()
    lower = jnp.full((8, TILE), bounds[0]) - 3.0
    cutoff = jnp.full((8, TILE), bounds[1]) - 0.5
    upper = jnp.full((8, TILE), bounds[2]) + 3.0
    half_width = (upper - cutoff) / 2.0
    center = (upper + cutoff) / 2.0
    sigma_one = half_width / (lower - center)
    sigma_two = 1.0 / (2.0 / sigma_one - sigma_one)
    coef[0] = center
    coef[1] = sigma_one / half_width
    coef[2] = 2.0 * sigma_two / half_width
    coef[3] = sigma_one * sigma_two

    for ext in (e0, e1):
        @pl.when(s == 0)
        def _():
            ext[:HB] = jnp.zeros((HB, NORB_DEV, TILE), BF16)

        @pl.when(s == N_SLAB - 1)
        def _():
            ext[HB + BLOCKS:] = jnp.zeros((HB, NORB_DEV, TILE), BF16)

    seg[EXTRA] = jnp.zeros((NORB_DEV, TILE), F32)

    loads[2].wait()
    wait_bytes(e0.at[pl.ds(HB, BLOCKS)], in_sem.at[5])
    pl.semaphore_wait(barrier, 4 + (CHIPS - 1) + NZ + 8 + 32)

    def send(src, dst, send_sem, recv_sem, to):
        pltpu.make_async_remote_copy(
            src_ref=src, dst_ref=dst, send_sem=send_sem, recv_sem=recv_sem,
            device_id=to, device_id_type=MESH,
        ).start()

    low_edge, high_edge = pl.ds(0, HB), pl.ds(HB + BLOCKS, HB)

    def send_edges(ext, which):
        @pl.when(not_last)
        def _():
            send(ext.at[pl.ds(BLOCKS, HB)], ext.at[low_edge],
                 h_send.at[which, 0], h_recv.at[which, 0], (s_up, o))

        @pl.when(not_first)
        def _():
            send(ext.at[pl.ds(HB, HB)], ext.at[high_edge],
                 h_send.at[which, 1], h_recv.at[which, 1], (s_down, o))

    def wait_edges(ext, which):
        @pl.when(not_first)
        def _():
            wait_bytes(ext.at[low_edge], h_recv.at[which, 0])

        @pl.when(not_last)
        def _():
            wait_bytes(ext.at[high_edge], h_recv.at[which, 1])

    send_edges(e0, 0)

    def rotation_columns(to_core, step, to_z):
        return rv.at[:, aligned(column_group(to_core, half, step, to_z), TILE)]

    def z_step(i, carry):
        step = jnp.where(i == 0, turn_of, i + 1)
        pltpu.make_async_copy(
            rotation_columns(core, step, z), rb.at[step, core, chip], z_recv.at[step]
        ).start()

        def one(j, inner):
            there = lax.rem(z * 2 + core + j, 2 * NZ)
            send(
                rotation_columns(lax.rem(there, 2), step, there // 2),
                rb.at[step, core, chip], z_send, z_recv.at[step], (s, x * 2 * NZ + there),
            )
            return inner

        lax.fori_loop(1, 2 * NZ, one, 0)
        return carry

    lax.fori_loop(0, STEPS - 1, z_step, 0)

    def of_x(step, at_x):
        return rb.at[step, :, pl.ds(at_x * NZ, NZ)]

    def of_x_core(step, at_core, at_x):
        return rb.at[step, at_core, pl.ds(at_x * NZ, NZ)]

    def orb_at(at_x):
        return (at_x * NZ + z) * 2 + core

    def to_slabs(step, at_x):
        low, high = of_x_core(step, 0, at_x), of_x_core(step, 1, at_x)
        send(low, low, y_send, y_recv, (s_two_up, o))
        send(high, high, y_send, y_recv, (s_two_down, o))

    def stage_one(step):
        mine = of_x(step, x)
        wait_bytes(mine, z_recv.at[step])
        send(mine, mine, x_send, x_recv.at[step, 0], (s, orb_at(x_up)))
        send(mine, mine, x_send, x_recv.at[step, 1], (s, orb_at(x_down)))

    def stage_two(step):
        wait_bytes(of_x(step, x_down), x_recv.at[step, 0])
        relayed = of_x_core(step, 0, x_down)
        send(relayed, relayed, x_send, x_recv.at[step, 2], (s, orb_at(x_up)))
        wait_bytes(of_x(step, x_up), x_recv.at[step, 1])
        relayed = of_x_core(step, 1, x_up)
        send(relayed, relayed, x_send, x_recv.at[step, 3], (s, orb_at(x_down)))

    def stage_three(step):
        wait_bytes(of_x_core(step, 0, x_far), x_recv.at[step, 2])
        wait_bytes(of_x_core(step, 1, x_far), x_recv.at[step, 3])

    table_copies = [
        pltpu.make_async_copy(t_made.at[pl.ds(i, 1)], to, t_sem.at[i])
        for i, to in enumerate((col_at, which_at, goes_on_at, last_at))
    ]

    def make_table():
        listed = (TILES, TILES)
        down = lax.broadcasted_iota(jnp.int32, listed, 0)
        along = lax.broadcasted_iota(jnp.int32, listed, 1)
        row_along = jnp.broadcast_to(t_rows[...], listed)
        col_along = jnp.broadcast_to(t_cols[...] + HB, listed)
        row_down = jnp.sum(jnp.where(down == along, row_along, 0), axis=1, keepdims=True)
        col_down = jnp.sum(jnp.where(down == along, col_along, 0), axis=1, keepdims=True)
        same_before = (row_along == row_down) & (along < down) & (along >= BLOCKS)
        before = same_before | ((row_along < row_down) & (along >= BLOCKS))
        place = jnp.sum(jnp.where(before, 1, 0), axis=1, keepdims=True)
        goes_on = jnp.minimum(jnp.sum(jnp.where(same_before, 1, 0), axis=1, keepdims=True), 1)
        here = (place == along) & (down >= BLOCKS)

        def in_order(values):
            return jnp.sum(jnp.where(here, values, 0), axis=0, keepdims=True)

        is_extra = down >= BLOCKS
        up_to = jnp.sum(jnp.where(is_extra & (row_down <= along), 1, 0), axis=0, keepdims=True)
        below = jnp.sum(jnp.where(is_extra & (row_down < along), 1, 0), axis=0, keepdims=True)
        t_made[0:1] = in_order(col_down)
        t_made[1:2] = in_order(down - BLOCKS)
        t_made[2:3] = in_order(goes_on)
        t_made[3:4] = jnp.where(up_to > below, up_to - 1, EXTRA)
        for made in table_copies:
            made.start()

    def times_tile(rows, tile):
        return lax.dot_general(rows, tile, (((1,), (1,)), ((), ())), preferred_element_type=F32)

    def apply_diagonal(ext):
        def body(i, carry):
            for u in range(UNROLL):
                b = i * UNROLL + u
                acc[b] = times_tile(ext[b + HB], diag[b])
            return carry

        lax.fori_loop(0, BLOCKS // UNROLL, body, 0)

    def apply_extra(ext):
        def multiply(i, carry):
            for u in range(UNROLL):
                m = i * UNROLL + u
                seg[m] = times_tile(ext[col_at[0, m]], extra[which_at[0, m]])
            return carry

        lax.fori_loop(0, EXTRA // UNROLL, multiply, 0)

        def add_up(i, run):
            for u in range(UNROLL):
                m = i * UNROLL + u
                run = seg[m] + goes_on_at[0, m].astype(F32) * run
                seg[m] = run
            return run

        lax.fori_loop(0, EXTRA // UNROLL, add_up, jnp.zeros((NORB_DEV, TILE), F32))

    lanes = lax.broadcasted_iota(jnp.int32, (1, TILE), 1)

    def filtered_first(b):
        total = acc[b] + seg[last_at[0, b]]
        source = e0[b + HB].astype(F32)
        value = (total - coef[0, 0:1] * source) * coef[1, 0:1]
        e1[b + HB] = jnp.where(lanes < counts[b], value, 0.0).astype(BF16)

    def filtered_second(b):
        total = acc[b] + seg[last_at[0, b]]
        source = e0[b + HB].astype(F32)
        first = e1[b + HB].astype(F32)
        value = (total - coef[0, 0:1] * first) * coef[2, 0:1] - coef[3, 0:1] * source
        return jnp.where(lanes < counts[b], value, 0.0).astype(BF16)

    loads[0].wait()
    loads[5].wait()
    make_table()
    loads[3].wait()
    apply_diagonal(e0)
    loads[4].wait()
    for made in table_copies:
        made.wait()
    loads[6].wait()
    wait_edges(e0, 0)
    apply_extra(e0)
    for b in (0, 1, BLOCKS - 2, BLOCKS - 1):
        filtered_first(b)
    send_edges(e1, 1)

    def inner_first(i, carry):
        for u in range(4):
            filtered_first(HB + 4 * i + u)
        return carry

    lax.fori_loop(0, (BLOCKS - 2 * HB) // 4, inner_first, 0)
    apply_diagonal(e1)
    stage_one(turn_of)
    to_slabs(turn_of, x)
    wait_edges(e1, 1)
    apply_extra(e1)
    stage_one(2)

    def destination(i):
        return lax.rem(x + i // NZ, NX) * NZ + lax.rem(z + lax.rem(i, NZ), NZ)

    def f_one(i, carry):
        there = destination(i)
        f2[there, :, :TILE] = filtered_second(2 * there)
        f2[there, :, TILE:] = filtered_second(2 * there + 1)

        @pl.when(i > 0)
        def _():
            send(f2.at[there], fb.at[core, chip, :, pl.ds(0, PAIR)], f_send, f_recv.at[x], (s, there * 2 + core))

        @pl.when(i == 0)
        def _():
            pltpu.make_async_copy(f2.at[there], fb.at[core, chip, :, pl.ds(0, PAIR)], f_recv.at[x]).start()

        return carry

    lax.fori_loop(0, CHIPS, f_one, 0)

    def turn(at_core, at_x, first_row):
        for group in range(2):
            block = fb[at_core, pl.ds(at_x * NZ + 4 * group, 4), :, first_row:first_row + TILE]
            k = at_core * (CHIPS * NORB_DEV) + (at_x * 2 + group) * TILE
            ft[first_row:first_row + TILE, aligned(k // TILE, TILE)] = block.reshape(TILE, TILE).T

    def pass_on(at_x):
        at = pl.ds(at_x * NZ, NZ)
        got = fb.at[core, at, :, pl.ds(0, PAIR)]
        wait_bytes(got, f_recv.at[at_x])
        send(fb.at[core, at, :, pl.ds(0, TILE)], fb.at[core, at, :, pl.ds(PAIR, TILE)],
             g_send, g_recv.at[at_x, 1], (s_up, o))
        send(fb.at[core, at, :, pl.ds(TILE, TILE)], fb.at[core, at, :, pl.ds(PAIR + TILE, TILE)],
             g_send, g_recv.at[at_x, 2], (s_down, o))
        send(got, got, g_send, g_recv.at[at_x, 0], (s, partner))
        turn(core, at_x, 0)
        turn(core, at_x, TILE)

    def relay(at_x):
        at = pl.ds(at_x * NZ, NZ)
        for side in range(2):
            wait_bytes(fb.at[core, at, :, pl.ds(PAIR + side * TILE, TILE)], g_recv.at[at_x, 1 + side])
        got = fb.at[core, at, :, pl.ds(PAIR, PAIR)]
        send(got, got, g_send, g_recv.at[at_x, 3], (s, partner))
        turn(core, at_x, PAIR)
        turn(core, at_x, PAIR + TILE)

    def take(at_x, part, which):
        at = pl.ds(at_x * NZ, NZ)
        wait_bytes(fb.at[1 - core, at, :, pl.ds(part * PAIR, PAIR)], g_recv.at[at_x, which])
        turn(1 - core, at_x, part * PAIR)
        turn(1 - core, at_x, part * PAIR + TILE)

    def back_x(i):
        return lax.rem(x + NX - i, NX)

    stage_two(turn_of)
    to_slabs(turn_of, x_down)
    to_slabs(turn_of, x_up)
    pass_on(back_x(0))
    stage_one(3)
    stage_two(2)
    stage_three(turn_of)
    to_slabs(turn_of, x_far)
    pass_on(back_x(1))
    relay(back_x(0))
    pass_on(back_x(2))
    relay(back_x(1))
    stage_two(3)
    pass_on(back_x(3))
    relay(back_x(2))
    stage_three(2)
    for i in range(NX):
        take(back_x(i), 0, 0)

    own = pl.ds(pl.multiple_of(chip * PAIR, PAIR), PAIR)
    low = pl.ds(pl.multiple_of(chip * PAIR, TILE), TILE)
    high = pl.ds(pl.multiple_of(chip * PAIR + TILE, TILE), TILE)

    def multiply(step, part):
        slot = rb[step].reshape(N_ORB * NORB_DEV, TILE)
        made = jnp.dot(ft[part * PAIR:(part + 1) * PAIR], slot, preferred_element_type=F32)
        ob[step, :, part * PAIR:(part + 1) * PAIR] = made.T.astype(BF16)

    def rotate_own(step):
        multiply(step, 0)
        first = column_group(core, half, step, z) * 4
        for i in range(4):
            owner = first + i
            piece = ob.at[step, pl.ds(i * NORB_DEV, NORB_DEV), pl.ds(0, PAIR)]

            @pl.when(owner == o)
            def _():
                pltpu.make_async_copy(piece, out.at[:, own], o_recv).start()

            @pl.when(owner != o)
            def _():
                send(piece, out.at[:, own], o_send, o_recv, (s, owner))

    def rotate_near(step):
        multiply(step, 1)
        first = column_group(core, half, step, z) * 4
        for i in range(4):
            rows = pl.ds(i * NORB_DEV, NORB_DEV)
            send(ob.at[step, rows, pl.ds(PAIR, TILE)], out.at[:, low], o_send, o_recv, (s_down, first + i))
            send(ob.at[step, rows, pl.ds(PAIR + TILE, TILE)], out.at[:, high], o_send, o_recv, (s_up, first + i))

    rotate_own(turn_of)
    rotate_own(2)
    relay(back_x(3))
    stage_three(3)
    rotate_own(3)
    wait_bytes(rb.at[1 - turn_of], y_recv)
    rotate_own(1 - turn_of)
    for i in range(NX):
        take(back_x(i), 1, 3)
    for step in (turn_of, 2, 3, 1 - turn_of):
        rotate_near(step)

    for which, ext in ((0, e0), (1, e1)):
        @pl.when(not_last)
        def _():
            wait_bytes(ext.at[low_edge], h_send.at[which, 0])

        @pl.when(not_first)
        def _():
            wait_bytes(ext.at[high_edge], h_send.at[which, 1])

    wait_bytes(rb.at[pl.ds(0, 3), 0, pl.ds(0, 15)], z_send)
    wait_bytes(rb.at[pl.ds(0, 3), :, pl.ds(0, 24)], x_send)
    wait_bytes(rb.at[0], y_send)
    wait_bytes(f2.at[pl.ds(0, CHIPS - 1)], f_send)
    wait_bytes(fb.at[:, :, :, pl.ds(0, PAIR + TILE)], g_send)
    mine_too = (x // 2 == core) & (lax.rem(z // 2, 2) == half)

    @pl.when(mine_too)
    def _():
        wait_bytes(f2.at[pl.ds(0, CHIPS - 1)], o_send)

    @pl.when(jnp.logical_not(mine_too))
    def _():
        wait_bytes(f2, o_send)

    wait_bytes(out, o_recv)


def local(orbitals_t, tiles, tile_rows, tile_cols, row_counts, bounds, rotation):
    dma = pltpu.SemaphoreType.DMA
    ext = pltpu.VMEM((BLOCKS + 2 * HB, NORB_DEV, TILE), BF16)
    anywhere = pl.BlockSpec(memory_space=pl.ANY)
    return pl.pallas_call(
        kernel,
        out_shape=jax.ShapeDtypeStruct(orbitals_t.shape, BF16),
        in_specs=[anywhere] * 7,
        out_specs=anywhere,
        scratch_shapes=[
            *[pltpu.VMEM((1, TILES), jnp.int32)] * 2,
            pltpu.VMEM((8, TILES), jnp.int32),
            *[pltpu.SMEM((1, TILES), jnp.int32)] * 4,
            pltpu.SMEM((BLOCKS,), jnp.int32),
            pltpu.SMEM((3,), F32),
            ext, ext,
            pltpu.VMEM((BLOCKS, TILE, TILE), BF16),
            pltpu.VMEM((EXTRA, TILE, TILE), BF16),
            pltpu.VMEM((BLOCKS, NORB_DEV, TILE), F32),
            pltpu.VMEM((EXTRA + 1, NORB_DEV, TILE), F32),
            pltpu.VMEM((4, 8, TILE), F32),
            pltpu.VMEM((CHIPS, NORB_DEV, PAIR), BF16),
            pltpu.VMEM((NORB_DEV, N_ORB * NORB_DEV), BF16),
            pltpu.VMEM((STEPS, 2, CHIPS, NORB_DEV, TILE), BF16),
            pltpu.VMEM((2, CHIPS, NORB_DEV, 2 * PAIR), BF16),
            pltpu.VMEM((2 * PAIR, N_ORB * NORB_DEV), BF16),
            pltpu.VMEM((STEPS, TILE, 2 * PAIR), BF16),
            dma((8,)), dma((4,)), dma((2, 2)), dma((2, 2)), dma, dma((STEPS,)), dma, dma((STEPS, 4)), dma, dma,
            dma, dma((NX,)), dma, dma((NX, 4)), dma, dma,
        ],
        compiler_params=pltpu.CompilerParams(
            collective_id=0, has_side_effects=True, vmem_limit_bytes=40 << 20
        ),
    )(
        *(pltpu.with_memory_space_constraint(v, pltpu.HBM) for v in (
            tile_rows.reshape(1, TILES), tile_cols.reshape(1, TILES), row_counts, bounds, orbitals_t, tiles, rotation,
        ))
    )


def solution(mesh):
    return jax.shard_map(
        local,
        mesh=mesh,
        in_specs=(
            P("orb", "slab"),
            P("slab", None, None),
            P("slab"),
            P("slab"),
            P("slab"),
            P(),
            P("orb", None),
        ),
        out_specs=P("orb", "slab"),
        check_vma=False,
    )
```

```python
import jax
import jax.numpy as jnp
from jax import lax
from jax.experimental import pallas as pl
from jax.experimental.pallas import tpu as pltpu
from jax.sharding import PartitionSpec as P

HB = 2
NX, NZ = 4, 8
CHIPS = NX * NZ
N_SLAB = 8
N_ORB = 2 * CHIPS
NORB_DEV = 32
TILE = 128
PAIR = 2 * TILE
BLOCKS = 64
EXTRA = 48
TILES = BLOCKS + EXTRA
ROWS_DEV = BLOCKS * TILE
STEPS = 4
UNROLL = 8
MESH = pl.DeviceIdType.MESH
BF16, F32 = jnp.bfloat16, jnp.float32


def column_group(core, half, step, z):
    owner_x = 2 * core + lax.rem(step + z, 2)
    z_pair = half + 2 * lax.rem(step // 2 + z // 2, 2)
    return owner_x * 4 + z_pair


def aligned(index, size):
    return pl.ds(pl.multiple_of(index * size, size), size)


def kernel(
    rows_hbm, cols_hbm, counts_hbm, bounds_hbm, orb_hbm, tiles_hbm, r_hbm, out,
    t_rows, t_cols, t_made, col_at, which_at, goes_on_at, last_at, counts, bounds, e0, e1, diag, extra, acc, seg, coef, f2, rv, rb, fb, ft, ob,
    in_sem, t_sem, h_send, h_recv, z_send, z_recv, x_send, x_recv, y_send, y_recv,
    f_send, f_recv, g_send, g_recv, o_send, o_recv,
):
    s, o = lax.axis_index("slab"), lax.axis_index("orb")
    core, chip = lax.rem(o, 2), o // 2
    z, x = lax.rem(chip, NZ), chip // NZ
    half = lax.rem(s, 2)
    partner = o + 1 - 2 * core
    x_up, x_down = lax.rem(x + 1, NX), lax.rem(x + NX - 1, NX)
    x_far = lax.rem(x + 2, NX)
    turn_of = lax.rem(s // 2, 2)
    s_two_up, s_two_down = lax.rem(s + 2, N_SLAB), lax.rem(s + N_SLAB - 2, N_SLAB)
    s_up, s_down = lax.rem(s + 1, N_SLAB), lax.rem(s + N_SLAB - 1, N_SLAB)
    not_first, not_last = s > 0, s < N_SLAB - 1

    loads = [
        pltpu.make_async_copy(rows_hbm, t_rows, in_sem.at[0]),
        pltpu.make_async_copy(bounds_hbm, bounds, in_sem.at[4]),
        pltpu.make_async_copy(r_hbm, rv, in_sem.at[1]),
        pltpu.make_async_copy(tiles_hbm.at[pl.ds(0, BLOCKS)], diag, in_sem.at[2]),
        pltpu.make_async_copy(tiles_hbm.at[pl.ds(BLOCKS, EXTRA)], extra, in_sem.at[3]),
        pltpu.make_async_copy(cols_hbm, t_cols, in_sem.at[6]),
        pltpu.make_async_copy(counts_hbm, counts, in_sem.at[7]),
    ]
    for load in loads:
        load.start()

    def load_block(b, carry):
        pltpu.make_async_copy(orb_hbm.at[:, aligned(b, TILE)], e0.at[HB + b], in_sem.at[5]).start()
        return carry

    lax.fori_loop(0, BLOCKS, load_block, 0)

    def wait_bytes(ref, sem):
        pltpu.make_async_copy(ref, ref, sem).wait()

    barrier = pltpu.get_barrier_semaphore()

    same_parity = lax.rem(z // 2, 2) == half

    def signal(to):
        pl.semaphore_signal(barrier, inc=1, device_id=to, device_id_type=MESH)

    def greet_chip(i, carry):
        signal((s, lax.rem(chip + i, CHIPS) * 2 + core))
        return carry

    def greet_column(i, carry):
        signal((s, (x * NZ + i) * 2 + 1 - core))
        return carry

    def greet_other(i, carry):
        signal((s, lax.rem(chip + i, CHIPS) * 2 + 1 - core))
        return carry

    def greet_near(i, carry):
        for near in (s_up, s_down):
            signal((near, lax.rem(chip + i, CHIPS) * 2 + x // 2))
        return carry

    for near in (s_up, s_down, s_two_up, s_two_down):
        signal((near, o))
    lax.fori_loop(1, CHIPS, greet_chip, 0)
    lax.fori_loop(0, NZ, greet_column, 0)
    lax.fori_loop(0, jnp.where(same_parity & (core != x // 2), CHIPS, 0), greet_other, 0)
    lax.fori_loop(0, jnp.where(same_parity, 0, CHIPS), greet_near, 0)

    loads[1].wait()
    lower = jnp.full((8, TILE), bounds[0]) - 3.0
    cutoff = jnp.full((8, TILE), bounds[1]) - 0.5
    upper = jnp.full((8, TILE), bounds[2]) + 3.0
    half_width = (upper - cutoff) / 2.0
    center = (upper + cutoff) / 2.0
    sigma_one = half_width / (lower - center)
    sigma_two = 1.0 / (2.0 / sigma_one - sigma_one)
    coef[0] = center
    coef[1] = sigma_one / half_width
    coef[2] = 2.0 * sigma_two / half_width
    coef[3] = sigma_one * sigma_two

    for ext in (e0, e1):
        @pl.when(s == 0)
        def _():
            ext[:HB] = jnp.zeros((HB, NORB_DEV, TILE), BF16)

        @pl.when(s == N_SLAB - 1)
        def _():
            ext[HB + BLOCKS:] = jnp.zeros((HB, NORB_DEV, TILE), BF16)

    seg[EXTRA] = jnp.zeros((NORB_DEV, TILE), F32)

    table_copies = [
        pltpu.make_async_copy(t_made.at[pl.ds(i, 1)], to, t_sem.at[i])
        for i, to in enumerate((col_at, which_at, goes_on_at, last_at))
    ]

    def make_table():
        listed = (TILES, TILES)
        down = lax.broadcasted_iota(jnp.int32, listed, 0)
        along = lax.broadcasted_iota(jnp.int32, listed, 1)
        row_along = jnp.broadcast_to(t_rows[...], listed)
        col_along = jnp.broadcast_to(t_cols[...] + HB, listed)
        row_down = jnp.sum(jnp.where(down == along, row_along, 0), axis=1, keepdims=True)
        col_down = jnp.sum(jnp.where(down == along, col_along, 0), axis=1, keepdims=True)
        same_before = (row_along == row_down) & (along < down) & (along >= BLOCKS)
        before = same_before | ((row_along < row_down) & (along >= BLOCKS))
        place = jnp.sum(jnp.where(before, 1, 0), axis=1, keepdims=True)
        goes_on = jnp.minimum(jnp.sum(jnp.where(same_before, 1, 0), axis=1, keepdims=True), 1)
        here = (place == along) & (down >= BLOCKS)

        def in_order(values):
            return jnp.sum(jnp.where(here, values, 0), axis=0, keepdims=True)

        is_extra = down >= BLOCKS
        up_to = jnp.sum(jnp.where(is_extra & (row_down <= along), 1, 0), axis=0, keepdims=True)
        below = jnp.sum(jnp.where(is_extra & (row_down < along), 1, 0), axis=0, keepdims=True)
        t_made[0:1] = in_order(col_down)
        t_made[1:2] = in_order(down - BLOCKS)
        t_made[2:3] = in_order(goes_on)
        t_made[3:4] = jnp.where(up_to > below, up_to - 1, EXTRA)
        for made in table_copies:
            made.start()

    def times_tile(rows, tile):
        return lax.dot_general(rows, tile, (((1,), (1,)), ((), ())), preferred_element_type=F32)

    def apply_diagonal(ext):
        def body(i, carry):
            for u in range(UNROLL):
                b = i * UNROLL + u
                acc[b] = times_tile(ext[b + HB], diag[b])
            return carry

        lax.fori_loop(0, BLOCKS // UNROLL, body, 0)

    loads[0].wait()
    loads[5].wait()
    make_table()
    wait_bytes(e0.at[pl.ds(HB, BLOCKS)], in_sem.at[5])
    loads[3].wait()
    apply_diagonal(e0)
    loads[2].wait()
    pl.semaphore_wait(barrier, 4 + (CHIPS - 1) + NZ + 8 + 32)

    def send(src, dst, send_sem, recv_sem, to):
        pltpu.make_async_remote_copy(
            src_ref=src, dst_ref=dst, send_sem=send_sem, recv_sem=recv_sem,
            device_id=to, device_id_type=MESH,
        ).start()

    low_edge, high_edge = pl.ds(0, HB), pl.ds(HB + BLOCKS, HB)

    def send_edges(ext, which):
        @pl.when(not_last)
        def _():
            send(ext.at[pl.ds(BLOCKS, HB)], ext.at[low_edge],
                 h_send.at[which, 0], h_recv.at[which, 0], (s_up, o))

        @pl.when(not_first)
        def _():
            send(ext.at[pl.ds(HB, HB)], ext.at[high_edge],
                 h_send.at[which, 1], h_recv.at[which, 1], (s_down, o))

    def wait_edges(ext, which):
        @pl.when(not_first)
        def _():
            wait_bytes(ext.at[low_edge], h_recv.at[which, 0])

        @pl.when(not_last)
        def _():
            wait_bytes(ext.at[high_edge], h_recv.at[which, 1])

    send_edges(e0, 0)

    def rotation_columns(to_core, step, to_z):
        return rv.at[:, aligned(column_group(to_core, half, step, to_z), TILE)]

    def z_step(i, carry):
        step = jnp.where(i == 0, turn_of, i + 1)
        pltpu.make_async_copy(
            rotation_columns(core, step, z), rb.at[step, core, chip], z_recv.at[step]
        ).start()

        def one(j, inner):
            there = lax.rem(z * 2 + core + j, 2 * NZ)
            send(
                rotation_columns(lax.rem(there, 2), step, there // 2),
                rb.at[step, core, chip], z_send, z_recv.at[step], (s, x * 2 * NZ + there),
            )
            return inner

        lax.fori_loop(1, 2 * NZ, one, 0)
        return carry

    lax.fori_loop(0, STEPS - 1, z_step, 0)

    def of_x(step, at_x):
        return rb.at[step, :, pl.ds(at_x * NZ, NZ)]

    def of_x_core(step, at_core, at_x):
        return rb.at[step, at_core, pl.ds(at_x * NZ, NZ)]

    def orb_at(at_x):
        return (at_x * NZ + z) * 2 + core

    def to_slabs(step, at_x):
        low, high = of_x_core(step, 0, at_x), of_x_core(step, 1, at_x)
        send(low, low, y_send, y_recv, (s_two_up, o))
        send(high, high, y_send, y_recv, (s_two_down, o))

    def stage_one(step):
        mine = of_x(step, x)
        wait_bytes(mine, z_recv.at[step])
        send(mine, mine, x_send, x_recv.at[step, 0], (s, orb_at(x_up)))
        send(mine, mine, x_send, x_recv.at[step, 1], (s, orb_at(x_down)))

    def stage_two(step):
        wait_bytes(of_x(step, x_down), x_recv.at[step, 0])
        relayed = of_x_core(step, 0, x_down)
        send(relayed, relayed, x_send, x_recv.at[step, 2], (s, orb_at(x_up)))
        wait_bytes(of_x(step, x_up), x_recv.at[step, 1])
        relayed = of_x_core(step, 1, x_up)
        send(relayed, relayed, x_send, x_recv.at[step, 3], (s, orb_at(x_down)))

    def stage_three(step):
        wait_bytes(of_x_core(step, 0, x_far), x_recv.at[step, 2])
        wait_bytes(of_x_core(step, 1, x_far), x_recv.at[step, 3])

    def apply_extra(ext):
        def multiply(i, carry):
            for u in range(UNROLL):
                m = i * UNROLL + u
                seg[m] = times_tile(ext[col_at[0, m]], extra[which_at[0, m]])
            return carry

        lax.fori_loop(0, EXTRA // UNROLL, multiply, 0)

        def add_up(i, run):
            for u in range(UNROLL):
                m = i * UNROLL + u
                run = seg[m] + goes_on_at[0, m].astype(F32) * run
                seg[m] = run
            return run

        lax.fori_loop(0, EXTRA // UNROLL, add_up, jnp.zeros((NORB_DEV, TILE), F32))

    lanes = lax.broadcasted_iota(jnp.int32, (1, TILE), 1)

    def filtered_first(b):
        total = acc[b] + seg[last_at[0, b]]
        source = e0[b + HB].astype(F32)
        value = (total - coef[0, 0:1] * source) * coef[1, 0:1]
        e1[b + HB] = jnp.where(lanes < counts[b], value, 0.0).astype(BF16)

    def filtered_second(b):
        total = acc[b] + seg[last_at[0, b]]
        source = e0[b + HB].astype(F32)
        first = e1[b + HB].astype(F32)
        value = (total - coef[0, 0:1] * first) * coef[2, 0:1] - coef[3, 0:1] * source
        return jnp.where(lanes < counts[b], value, 0.0).astype(BF16)

    loads[4].wait()
    for made in table_copies:
        made.wait()
    loads[6].wait()
    wait_edges(e0, 0)
    apply_extra(e0)
    for b in (0, 1, BLOCKS - 2, BLOCKS - 1):
        filtered_first(b)
    send_edges(e1, 1)

    def inner_first(i, carry):
        for u in range(4):
            filtered_first(HB + 4 * i + u)
        return carry

    lax.fori_loop(0, (BLOCKS - 2 * HB) // 4, inner_first, 0)
    apply_diagonal(e1)
    stage_one(turn_of)
    to_slabs(turn_of, x)
    wait_edges(e1, 1)
    apply_extra(e1)
    stage_one(2)

    def destination(i):
        return lax.rem(x + i // NZ, NX) * NZ + lax.rem(z + lax.rem(i, NZ), NZ)

    def f_one(i, carry):
        there = destination(i)
        f2[there, :, :TILE] = filtered_second(2 * there)
        f2[there, :, TILE:] = filtered_second(2 * there + 1)

        @pl.when(i > 0)
        def _():
            send(f2.at[there], fb.at[core, chip, :, pl.ds(0, PAIR)], f_send, f_recv.at[x], (s, there * 2 + core))

        @pl.when(i == 0)
        def _():
            pltpu.make_async_copy(f2.at[there], fb.at[core, chip, :, pl.ds(0, PAIR)], f_recv.at[x]).start()

        return carry

    lax.fori_loop(0, CHIPS, f_one, 0)

    def turn(at_core, at_x, first_row):
        for group in range(2):
            block = fb[at_core, pl.ds(at_x * NZ + 4 * group, 4), :, first_row:first_row + TILE]
            k = at_core * (CHIPS * NORB_DEV) + (at_x * 2 + group) * TILE
            ft[first_row:first_row + TILE, aligned(k // TILE, TILE)] = block.reshape(TILE, TILE).T

    def pass_on(at_x):
        at = pl.ds(at_x * NZ, NZ)
        got = fb.at[core, at, :, pl.ds(0, PAIR)]
        wait_bytes(got, f_recv.at[at_x])
        send(fb.at[core, at, :, pl.ds(0, TILE)], fb.at[core, at, :, pl.ds(PAIR, TILE)],
             g_send, g_recv.at[at_x, 1], (s_up, o))
        send(fb.at[core, at, :, pl.ds(TILE, TILE)], fb.at[core, at, :, pl.ds(PAIR + TILE, TILE)],
             g_send, g_recv.at[at_x, 2], (s_down, o))
        send(got, got, g_send, g_recv.at[at_x, 0], (s, partner))
        turn(core, at_x, 0)
        turn(core, at_x, TILE)

    def relay(at_x):
        at = pl.ds(at_x * NZ, NZ)
        for side in range(2):
            wait_bytes(fb.at[core, at, :, pl.ds(PAIR + side * TILE, TILE)], g_recv.at[at_x, 1 + side])
        got = fb.at[core, at, :, pl.ds(PAIR, PAIR)]
        send(got, got, g_send, g_recv.at[at_x, 3], (s, partner))
        turn(core, at_x, PAIR)
        turn(core, at_x, PAIR + TILE)

    def take(at_x, part, which):
        at = pl.ds(at_x * NZ, NZ)
        wait_bytes(fb.at[1 - core, at, :, pl.ds(part * PAIR, PAIR)], g_recv.at[at_x, which])
        turn(1 - core, at_x, part * PAIR)
        turn(1 - core, at_x, part * PAIR + TILE)

    def back_x(i):
        return lax.rem(x + NX - i, NX)

    stage_two(turn_of)
    to_slabs(turn_of, x_down)
    to_slabs(turn_of, x_up)
    pass_on(back_x(0))
    stage_one(3)
    stage_two(2)
    stage_three(turn_of)
    to_slabs(turn_of, x_far)
    pass_on(back_x(1))
    relay(back_x(0))
    pass_on(back_x(2))
    relay(back_x(1))
    stage_two(3)
    pass_on(back_x(3))
    relay(back_x(2))
    stage_three(2)
    for i in range(NX):
        take(back_x(i), 0, 0)

    own = pl.ds(pl.multiple_of(chip * PAIR, PAIR), PAIR)
    low = pl.ds(pl.multiple_of(chip * PAIR, TILE), TILE)
    high = pl.ds(pl.multiple_of(chip * PAIR + TILE, TILE), TILE)

    def multiply(step, part):
        slot = rb[step].reshape(N_ORB * NORB_DEV, TILE)
        made = jnp.dot(ft[part * PAIR:(part + 1) * PAIR], slot, preferred_element_type=F32)
        ob[step, :, part * PAIR:(part + 1) * PAIR] = made.T.astype(BF16)

    def rotate_own(step):
        multiply(step, 0)
        first = column_group(core, half, step, z) * 4
        for i in range(4):
            owner = first + i
            piece = ob.at[step, pl.ds(i * NORB_DEV, NORB_DEV), pl.ds(0, PAIR)]

            @pl.when(owner == o)
            def _():
                pltpu.make_async_copy(piece, out.at[:, own], o_recv).start()

            @pl.when(owner != o)
            def _():
                send(piece, out.at[:, own], o_send, o_recv, (s, owner))

    def rotate_near(step):
        multiply(step, 1)
        first = column_group(core, half, step, z) * 4
        for i in range(4):
            rows = pl.ds(i * NORB_DEV, NORB_DEV)
            send(ob.at[step, rows, pl.ds(PAIR, TILE)], out.at[:, low], o_send, o_recv, (s_down, first + i))
            send(ob.at[step, rows, pl.ds(PAIR + TILE, TILE)], out.at[:, high], o_send, o_recv, (s_up, first + i))

    rotate_own(turn_of)
    rotate_own(2)
    relay(back_x(3))
    stage_three(3)
    rotate_own(3)
    wait_bytes(rb.at[1 - turn_of], y_recv)
    rotate_own(1 - turn_of)
    for i in range(NX):
        take(back_x(i), 1, 3)
    for step in (turn_of, 2, 3, 1 - turn_of):
        rotate_near(step)

    for which, ext in ((0, e0), (1, e1)):
        @pl.when(not_last)
        def _():
            wait_bytes(ext.at[low_edge], h_send.at[which, 0])

        @pl.when(not_first)
        def _():
            wait_bytes(ext.at[high_edge], h_send.at[which, 1])

    wait_bytes(rb.at[pl.ds(0, 3), 0, pl.ds(0, 15)], z_send)
    wait_bytes(rb.at[pl.ds(0, 3), :, pl.ds(0, 24)], x_send)
    wait_bytes(rb.at[0], y_send)
    wait_bytes(f2.at[pl.ds(0, CHIPS - 1)], f_send)
    wait_bytes(fb.at[:, :, :, pl.ds(0, PAIR + TILE)], g_send)
    mine_too = (x // 2 == core) & (lax.rem(z // 2, 2) == half)

    @pl.when(mine_too)
    def _():
        wait_bytes(f2.at[pl.ds(0, CHIPS - 1)], o_send)

    @pl.when(jnp.logical_not(mine_too))
    def _():
        wait_bytes(f2, o_send)

    wait_bytes(out, o_recv)


def local(orbitals_t, tiles, tile_rows, tile_cols, row_counts, bounds, rotation):
    dma = pltpu.SemaphoreType.DMA
    ext = pltpu.VMEM((BLOCKS + 2 * HB, NORB_DEV, TILE), BF16)
    anywhere = pl.BlockSpec(memory_space=pl.ANY)
    return pl.pallas_call(
        kernel,
        out_shape=jax.ShapeDtypeStruct(orbitals_t.shape, BF16),
        in_specs=[anywhere] * 7,
        out_specs=anywhere,
        scratch_shapes=[
            *[pltpu.VMEM((1, TILES), jnp.int32)] * 2,
            pltpu.VMEM((8, TILES), jnp.int32),
            *[pltpu.SMEM((1, TILES), jnp.int32)] * 4,
            pltpu.SMEM((BLOCKS,), jnp.int32),
            pltpu.SMEM((3,), F32),
            ext, ext,
            pltpu.VMEM((BLOCKS, TILE, TILE), BF16),
            pltpu.VMEM((EXTRA, TILE, TILE), BF16),
            pltpu.VMEM((BLOCKS, NORB_DEV, TILE), F32),
            pltpu.VMEM((EXTRA + 1, NORB_DEV, TILE), F32),
            pltpu.VMEM((4, 8, TILE), F32),
            pltpu.VMEM((CHIPS, NORB_DEV, PAIR), BF16),
            pltpu.VMEM((NORB_DEV, N_ORB * NORB_DEV), BF16),
            pltpu.VMEM((STEPS, 2, CHIPS, NORB_DEV, TILE), BF16),
            pltpu.VMEM((2, CHIPS, NORB_DEV, 2 * PAIR), BF16),
            pltpu.VMEM((2 * PAIR, N_ORB * NORB_DEV), BF16),
            pltpu.VMEM((STEPS, TILE, 2 * PAIR), BF16),
            dma((8,)), dma((4,)), dma((2, 2)), dma((2, 2)), dma, dma((STEPS,)), dma, dma((STEPS, 4)), dma, dma,
            dma, dma((NX,)), dma, dma((NX, 4)), dma, dma,
        ],
        compiler_params=pltpu.CompilerParams(
            collective_id=0, has_side_effects=True, vmem_limit_bytes=40 << 20
        ),
    )(
        *(pltpu.with_memory_space_constraint(v, pltpu.HBM) for v in (
            tile_rows.reshape(1, TILES), tile_cols.reshape(1, TILES), row_counts, bounds, orbitals_t, tiles, rotation,
        ))
    )


def solution(mesh):
    return jax.shard_map(
        local,
        mesh=mesh,
        in_specs=(
            P("orb", "slab"),
            P("slab", None, None),
            P("slab"),
            P("slab"),
            P("slab"),
            P(),
            P("orb", None),
        ),
        out_specs=P("orb", "slab"),
        check_vma=False,
    )
```

```python
import jax
import jax.numpy as jnp
from jax import lax
from jax.experimental import pallas as pl
from jax.experimental.pallas import tpu as pltpu
from jax.sharding import PartitionSpec as P

HB = 2
NX, NZ = 4, 8
CHIPS = NX * NZ
N_SLAB = 8
N_ORB = 2 * CHIPS
NORB_DEV = 32
TILE = 128
PAIR = 2 * TILE
BLOCKS = 64
EXTRA = 48
TILES = BLOCKS + EXTRA
ROWS_DEV = BLOCKS * TILE
STEPS = 4
UNROLL = 16
MESH = pl.DeviceIdType.MESH
BF16, F32 = jnp.bfloat16, jnp.float32


def column_group(core, half, step, z):
    owner_x = 2 * core + lax.rem(step + z, 2)
    z_pair = half + 2 * lax.rem(step // 2 + z // 2, 2)
    return owner_x * 4 + z_pair


def aligned(index, size):
    return pl.ds(pl.multiple_of(index * size, size), size)


def kernel(
    rows_hbm, cols_hbm, counts_hbm, bounds_hbm, orb_hbm, tiles_hbm, r_hbm, out,
    t_rows, t_cols, t_made, col_at, which_at, goes_on_at, last_at, counts, bounds, e0, e1, diag, extra, acc, seg, coef, f2, rv, rb, fb, ft, ob,
    in_sem, t_sem, h_send, h_recv, z_send, z_recv, x_send, x_recv, y_send, y_recv,
    f_send, f_recv, g_send, g_recv, o_send, o_recv,
):
    s, o = lax.axis_index("slab"), lax.axis_index("orb")
    core, chip = lax.rem(o, 2), o // 2
    z, x = lax.rem(chip, NZ), chip // NZ
    half = lax.rem(s, 2)
    partner = o + 1 - 2 * core
    x_up, x_down = lax.rem(x + 1, NX), lax.rem(x + NX - 1, NX)
    x_far = lax.rem(x + 2, NX)
    turn_of = lax.rem(s // 2, 2)
    s_two_up, s_two_down = lax.rem(s + 2, N_SLAB), lax.rem(s + N_SLAB - 2, N_SLAB)
    s_up, s_down = lax.rem(s + 1, N_SLAB), lax.rem(s + N_SLAB - 1, N_SLAB)
    not_first, not_last = s > 0, s < N_SLAB - 1

    loads = [
        pltpu.make_async_copy(rows_hbm, t_rows, in_sem.at[0]),
        pltpu.make_async_copy(bounds_hbm, bounds, in_sem.at[4]),
        pltpu.make_async_copy(r_hbm, rv, in_sem.at[1]),
        pltpu.make_async_copy(tiles_hbm.at[pl.ds(0, BLOCKS)], diag, in_sem.at[2]),
        pltpu.make_async_copy(tiles_hbm.at[pl.ds(BLOCKS, EXTRA)], extra, in_sem.at[3]),
        pltpu.make_async_copy(cols_hbm, t_cols, in_sem.at[6]),
        pltpu.make_async_copy(counts_hbm, counts, in_sem.at[7]),
    ]
    for load in loads:
        load.start()

    def load_block(b, carry):
        pltpu.make_async_copy(orb_hbm.at[:, aligned(b, TILE)], e0.at[HB + b], in_sem.at[5]).start()
        return carry

    lax.fori_loop(0, BLOCKS, load_block, 0)

    def wait_bytes(ref, sem):
        pltpu.make_async_copy(ref, ref, sem).wait()

    barrier = pltpu.get_barrier_semaphore()

    same_parity = lax.rem(z // 2, 2) == half

    def signal(to):
        pl.semaphore_signal(barrier, inc=1, device_id=to, device_id_type=MESH)

    def greet_chip(i, carry):
        signal((s, lax.rem(chip + i, CHIPS) * 2 + core))
        return carry

    def greet_column(i, carry):
        signal((s, (x * NZ + i) * 2 + 1 - core))
        return carry

    def greet_other(i, carry):
        signal((s, lax.rem(chip + i, CHIPS) * 2 + 1 - core))
        return carry

    def greet_near(i, carry):
        for near in (s_up, s_down):
            signal((near, lax.rem(chip + i, CHIPS) * 2 + x // 2))
        return carry

    for near in (s_up, s_down, s_two_up, s_two_down):
        signal((near, o))
    lax.fori_loop(1, CHIPS, greet_chip, 0)
    lax.fori_loop(0, NZ, greet_column, 0)
    lax.fori_loop(0, jnp.where(same_parity & (core != x // 2), CHIPS, 0), greet_other, 0)
    lax.fori_loop(0, jnp.where(same_parity, 0, CHIPS), greet_near, 0)

    loads[1].wait()
    lower = jnp.full((8, TILE), bounds[0]) - 3.0
    cutoff = jnp.full((8, TILE), bounds[1]) - 0.5
    upper = jnp.full((8, TILE), bounds[2]) + 3.0
    half_width = (upper - cutoff) / 2.0
    center = (upper + cutoff) / 2.0
    sigma_one = half_width / (lower - center)
    sigma_two = 1.0 / (2.0 / sigma_one - sigma_one)
    coef[0] = center
    coef[1] = sigma_one / half_width
    coef[2] = 2.0 * sigma_two / half_width
    coef[3] = sigma_one * sigma_two

    for ext in (e0, e1):
        @pl.when(s == 0)
        def _():
            ext[:HB] = jnp.zeros((HB, NORB_DEV, TILE), BF16)

        @pl.when(s == N_SLAB - 1)
        def _():
            ext[HB + BLOCKS:] = jnp.zeros((HB, NORB_DEV, TILE), BF16)

    seg[EXTRA] = jnp.zeros((NORB_DEV, TILE), F32)

    table_copies = [
        pltpu.make_async_copy(t_made.at[pl.ds(i, 1)], to, t_sem.at[i])
        for i, to in enumerate((col_at, which_at, goes_on_at, last_at))
    ]

    def make_table():
        listed = (TILES, TILES)
        down = lax.broadcasted_iota(jnp.int32, listed, 0)
        along = lax.broadcasted_iota(jnp.int32, listed, 1)
        row_along = jnp.broadcast_to(t_rows[...], listed)
        col_along = jnp.broadcast_to(t_cols[...] + HB, listed)
        row_down = jnp.sum(jnp.where(down == along, row_along, 0), axis=1, keepdims=True)
        col_down = jnp.sum(jnp.where(down == along, col_along, 0), axis=1, keepdims=True)
        same_before = (row_along == row_down) & (along < down) & (along >= BLOCKS)
        before = same_before | ((row_along < row_down) & (along >= BLOCKS))
        place = jnp.sum(jnp.where(before, 1, 0), axis=1, keepdims=True)
        goes_on = jnp.minimum(jnp.sum(jnp.where(same_before, 1, 0), axis=1, keepdims=True), 1)
        here = (place == along) & (down >= BLOCKS)

        def in_order(values):
            return jnp.sum(jnp.where(here, values, 0), axis=0, keepdims=True)

        is_extra = down >= BLOCKS
        up_to = jnp.sum(jnp.where(is_extra & (row_down <= along), 1, 0), axis=0, keepdims=True)
        below = jnp.sum(jnp.where(is_extra & (row_down < along), 1, 0), axis=0, keepdims=True)
        t_made[0:1] = in_order(col_down)
        t_made[1:2] = in_order(down - BLOCKS)
        t_made[2:3] = in_order(goes_on)
        t_made[3:4] = jnp.where(up_to > below, up_to - 1, EXTRA)
        for made in table_copies:
            made.start()

    def times_tile(rows, tile):
        return lax.dot_general(rows, tile, (((1,), (1,)), ((), ())), preferred_element_type=F32)

    def apply_diagonal(ext):
        def body(i, carry):
            for u in range(UNROLL):
                b = i * UNROLL + u
                acc[b] = times_tile(ext[b + HB], diag[b])
            return carry

        lax.fori_loop(0, BLOCKS // UNROLL, body, 0)

    loads[0].wait()
    loads[5].wait()
    make_table()
    wait_bytes(e0.at[pl.ds(HB, BLOCKS)], in_sem.at[5])
    loads[3].wait()
    apply_diagonal(e0)
    loads[2].wait()
    pl.semaphore_wait(barrier, 4 + (CHIPS - 1) + NZ + 8 + 32)

    def send(src, dst, send_sem, recv_sem, to):
        pltpu.make_async_remote_copy(
            src_ref=src, dst_ref=dst, send_sem=send_sem, recv_sem=recv_sem,
            device_id=to, device_id_type=MESH,
        ).start()

    low_edge, high_edge = pl.ds(0, HB), pl.ds(HB + BLOCKS, HB)

    def send_edges(ext, which):
        @pl.when(not_last)
        def _():
            send(ext.at[pl.ds(BLOCKS, HB)], ext.at[low_edge],
                 h_send.at[which, 0], h_recv.at[which, 0], (s_up, o))

        @pl.when(not_first)
        def _():
            send(ext.at[pl.ds(HB, HB)], ext.at[high_edge],
                 h_send.at[which, 1], h_recv.at[which, 1], (s_down, o))

    def wait_edges(ext, which):
        @pl.when(not_first)
        def _():
            wait_bytes(ext.at[low_edge], h_recv.at[which, 0])

        @pl.when(not_last)
        def _():
            wait_bytes(ext.at[high_edge], h_recv.at[which, 1])

    send_edges(e0, 0)

    def rotation_columns(to_core, step, to_z):
        return rv.at[:, aligned(column_group(to_core, half, step, to_z), TILE)]

    def z_step(i, carry):
        step = jnp.where(i == 0, turn_of, i + 1)
        pltpu.make_async_copy(
            rotation_columns(core, step, z), rb.at[step, core, chip], z_recv.at[step]
        ).start()

        def one(j, inner):
            there = lax.rem(z * 2 + core + j, 2 * NZ)
            send(
                rotation_columns(lax.rem(there, 2), step, there // 2),
                rb.at[step, core, chip], z_send, z_recv.at[step], (s, x * 2 * NZ + there),
            )
            return inner

        lax.fori_loop(1, 2 * NZ, one, 0)
        return carry

    lax.fori_loop(0, STEPS - 1, z_step, 0)

    def of_x(step, at_x):
        return rb.at[step, :, pl.ds(at_x * NZ, NZ)]

    def of_x_core(step, at_core, at_x):
        return rb.at[step, at_core, pl.ds(at_x * NZ, NZ)]

    def orb_at(at_x):
        return (at_x * NZ + z) * 2 + core

    def to_slabs(step, at_x):
        low, high = of_x_core(step, 0, at_x), of_x_core(step, 1, at_x)
        send(low, low, y_send, y_recv, (s_two_up, o))
        send(high, high, y_send, y_recv, (s_two_down, o))

    def stage_one(step):
        mine = of_x(step, x)
        wait_bytes(mine, z_recv.at[step])
        send(mine, mine, x_send, x_recv.at[step, 0], (s, orb_at(x_up)))
        send(mine, mine, x_send, x_recv.at[step, 1], (s, orb_at(x_down)))

    def stage_two(step):
        wait_bytes(of_x(step, x_down), x_recv.at[step, 0])
        relayed = of_x_core(step, 0, x_down)
        send(relayed, relayed, x_send, x_recv.at[step, 2], (s, orb_at(x_up)))
        wait_bytes(of_x(step, x_up), x_recv.at[step, 1])
        relayed = of_x_core(step, 1, x_up)
        send(relayed, relayed, x_send, x_recv.at[step, 3], (s, orb_at(x_down)))

    def stage_three(step):
        wait_bytes(of_x_core(step, 0, x_far), x_recv.at[step, 2])
        wait_bytes(of_x_core(step, 1, x_far), x_recv.at[step, 3])

    def apply_extra(ext):
        def multiply(i, carry):
            for u in range(UNROLL):
                m = i * UNROLL + u
                seg[m] = times_tile(ext[col_at[0, m]], extra[which_at[0, m]])
            return carry

        lax.fori_loop(0, EXTRA // UNROLL, multiply, 0)

        def add_up(i, run):
            for u in range(UNROLL):
                m = i * UNROLL + u
                run = seg[m] + goes_on_at[0, m].astype(F32) * run
                seg[m] = run
            return run

        lax.fori_loop(0, EXTRA // UNROLL, add_up, jnp.zeros((NORB_DEV, TILE), F32))

    lanes = lax.broadcasted_iota(jnp.int32, (1, TILE), 1)

    def filtered_first(b):
        total = acc[b] + seg[last_at[0, b]]
        source = e0[b + HB].astype(F32)
        value = (total - coef[0, 0:1] * source) * coef[1, 0:1]
        e1[b + HB] = jnp.where(lanes < counts[b], value, 0.0).astype(BF16)

    def filtered_second(b):
        total = acc[b] + seg[last_at[0, b]]
        source = e0[b + HB].astype(F32)
        first = e1[b + HB].astype(F32)
        value = (total - coef[0, 0:1] * first) * coef[2, 0:1] - coef[3, 0:1] * source
        return jnp.where(lanes < counts[b], value, 0.0).astype(BF16)

    loads[4].wait()
    for made in table_copies:
        made.wait()
    loads[6].wait()
    wait_edges(e0, 0)
    apply_extra(e0)
    for b in (0, 1, BLOCKS - 2, BLOCKS - 1):
        filtered_first(b)
    send_edges(e1, 1)

    def inner_first(i, carry):
        for u in range(4):
            filtered_first(HB + 4 * i + u)
        return carry

    lax.fori_loop(0, (BLOCKS - 2 * HB) // 4, inner_first, 0)
    apply_diagonal(e1)
    stage_one(turn_of)
    to_slabs(turn_of, x)
    wait_edges(e1, 1)
    apply_extra(e1)
    stage_one(2)

    def destination(i):
        return lax.rem(x + i // NZ, NX) * NZ + lax.rem(z + lax.rem(i, NZ), NZ)

    def f_one(i, carry):
        there = destination(i)
        f2[there, :, :TILE] = filtered_second(2 * there)
        f2[there, :, TILE:] = filtered_second(2 * there + 1)

        @pl.when(i > 0)
        def _():
            send(f2.at[there], fb.at[core, chip, :, pl.ds(0, PAIR)], f_send, f_recv.at[x], (s, there * 2 + core))

        @pl.when(i == 0)
        def _():
            pltpu.make_async_copy(f2.at[there], fb.at[core, chip, :, pl.ds(0, PAIR)], f_recv.at[x]).start()

        return carry

    lax.fori_loop(0, CHIPS, f_one, 0)

    def turn(at_core, at_x, first_row):
        for group in range(2):
            block = fb[at_core, pl.ds(at_x * NZ + 4 * group, 4), :, first_row:first_row + TILE]
            k = at_core * (CHIPS * NORB_DEV) + (at_x * 2 + group) * TILE
            ft[first_row:first_row + TILE, aligned(k // TILE, TILE)] = block.reshape(TILE, TILE).T

    def pass_on(at_x):
        at = pl.ds(at_x * NZ, NZ)
        got = fb.at[core, at, :, pl.ds(0, PAIR)]
        wait_bytes(got, f_recv.at[at_x])
        send(fb.at[core, at, :, pl.ds(0, TILE)], fb.at[core, at, :, pl.ds(PAIR, TILE)],
             g_send, g_recv.at[at_x, 1], (s_up, o))
        send(fb.at[core, at, :, pl.ds(TILE, TILE)], fb.at[core, at, :, pl.ds(PAIR + TILE, TILE)],
             g_send, g_recv.at[at_x, 2], (s_down, o))
        send(got, got, g_send, g_recv.at[at_x, 0], (s, partner))
        turn(core, at_x, 0)
        turn(core, at_x, TILE)

    def relay(at_x):
        at = pl.ds(at_x * NZ, NZ)
        for side in range(2):
            wait_bytes(fb.at[core, at, :, pl.ds(PAIR + side * TILE, TILE)], g_recv.at[at_x, 1 + side])
        got = fb.at[core, at, :, pl.ds(PAIR, PAIR)]
        send(got, got, g_send, g_recv.at[at_x, 3], (s, partner))
        turn(core, at_x, PAIR)
        turn(core, at_x, PAIR + TILE)

    def take(at_x, part, which):
        at = pl.ds(at_x * NZ, NZ)
        wait_bytes(fb.at[1 - core, at, :, pl.ds(part * PAIR, PAIR)], g_recv.at[at_x, which])
        turn(1 - core, at_x, part * PAIR)
        turn(1 - core, at_x, part * PAIR + TILE)

    def back_x(i):
        return lax.rem(x + NX - i, NX)

    stage_two(turn_of)
    to_slabs(turn_of, x_down)
    to_slabs(turn_of, x_up)
    pass_on(back_x(0))
    stage_one(3)
    stage_two(2)
    stage_three(turn_of)
    to_slabs(turn_of, x_far)
    pass_on(back_x(1))
    relay(back_x(0))
    pass_on(back_x(2))
    relay(back_x(1))
    stage_two(3)
    pass_on(back_x(3))
    relay(back_x(2))
    for i in range(NX):
        take(back_x(i), 0, 0)

    own = pl.ds(pl.multiple_of(chip * PAIR, PAIR), PAIR)
    low = pl.ds(pl.multiple_of(chip * PAIR, TILE), TILE)
    high = pl.ds(pl.multiple_of(chip * PAIR + TILE, TILE), TILE)

    def multiply(step, part):
        slot = rb[step].reshape(N_ORB * NORB_DEV, TILE)
        made = jnp.dot(ft[part * PAIR:(part + 1) * PAIR], slot, preferred_element_type=F32)
        ob[step, :, part * PAIR:(part + 1) * PAIR] = made.T.astype(BF16)

    def rotate_own(step):
        multiply(step, 0)
        first = column_group(core, half, step, z) * 4
        for i in range(4):
            owner = first + i
            piece = ob.at[step, pl.ds(i * NORB_DEV, NORB_DEV), pl.ds(0, PAIR)]

            @pl.when(owner == o)
            def _():
                pltpu.make_async_copy(piece, out.at[:, own], o_recv).start()

            @pl.when(owner != o)
            def _():
                send(piece, out.at[:, own], o_send, o_recv, (s, owner))

    def rotate_near(step):
        multiply(step, 1)
        first = column_group(core, half, step, z) * 4
        for i in range(4):
            rows = pl.ds(i * NORB_DEV, NORB_DEV)
            send(ob.at[step, rows, pl.ds(PAIR, TILE)], out.at[:, low], o_send, o_recv, (s_down, first + i))
            send(ob.at[step, rows, pl.ds(PAIR + TILE, TILE)], out.at[:, high], o_send, o_recv, (s_up, first + i))

    rotate_own(turn_of)
    relay(back_x(3))
    stage_three(2)
    rotate_own(2)
    stage_three(3)
    rotate_own(3)
    wait_bytes(rb.at[1 - turn_of], y_recv)
    rotate_own(1 - turn_of)
    for i in range(NX):
        take(back_x(i), 1, 3)
    for step in (turn_of, 2, 3, 1 - turn_of):
        rotate_near(step)

    for which, ext in ((0, e0), (1, e1)):
        @pl.when(not_last)
        def _():
            wait_bytes(ext.at[low_edge], h_send.at[which, 0])

        @pl.when(not_first)
        def _():
            wait_bytes(ext.at[high_edge], h_send.at[which, 1])

    wait_bytes(rb.at[pl.ds(0, 3), 0, pl.ds(0, 15)], z_send)
    wait_bytes(rb.at[pl.ds(0, 3), :, pl.ds(0, 24)], x_send)
    wait_bytes(rb.at[0], y_send)
    wait_bytes(f2.at[pl.ds(0, CHIPS - 1)], f_send)
    wait_bytes(fb.at[:, :, :, pl.ds(0, PAIR + TILE)], g_send)
    mine_too = (x // 2 == core) & (lax.rem(z // 2, 2) == half)

    @pl.when(mine_too)
    def _():
        wait_bytes(f2.at[pl.ds(0, CHIPS - 1)], o_send)

    @pl.when(jnp.logical_not(mine_too))
    def _():
        wait_bytes(f2, o_send)

    wait_bytes(out, o_recv)


def local(orbitals_t, tiles, tile_rows, tile_cols, row_counts, bounds, rotation):
    dma = pltpu.SemaphoreType.DMA
    ext = pltpu.VMEM((BLOCKS + 2 * HB, NORB_DEV, TILE), BF16)
    anywhere = pl.BlockSpec(memory_space=pl.ANY)
    return pl.pallas_call(
        kernel,
        out_shape=jax.ShapeDtypeStruct(orbitals_t.shape, BF16),
        in_specs=[anywhere] * 7,
        out_specs=anywhere,
        scratch_shapes=[
            *[pltpu.VMEM((1, TILES), jnp.int32)] * 2,
            pltpu.VMEM((8, TILES), jnp.int32),
            *[pltpu.SMEM((1, TILES), jnp.int32)] * 4,
            pltpu.SMEM((BLOCKS,), jnp.int32),
            pltpu.SMEM((3,), F32),
            ext, ext,
            pltpu.VMEM((BLOCKS, TILE, TILE), BF16),
            pltpu.VMEM((EXTRA, TILE, TILE), BF16),
            pltpu.VMEM((BLOCKS, NORB_DEV, TILE), F32),
            pltpu.VMEM((EXTRA + 1, NORB_DEV, TILE), F32),
            pltpu.VMEM((4, 8, TILE), F32),
            pltpu.VMEM((CHIPS, NORB_DEV, PAIR), BF16),
            pltpu.VMEM((NORB_DEV, N_ORB * NORB_DEV), BF16),
            pltpu.VMEM((STEPS, 2, CHIPS, NORB_DEV, TILE), BF16),
            pltpu.VMEM((2, CHIPS, NORB_DEV, 2 * PAIR), BF16),
            pltpu.VMEM((2 * PAIR, N_ORB * NORB_DEV), BF16),
            pltpu.VMEM((STEPS, TILE, 2 * PAIR), BF16),
            dma((8,)), dma((4,)), dma((2, 2)), dma((2, 2)), dma, dma((STEPS,)), dma, dma((STEPS, 4)), dma, dma,
            dma, dma((NX,)), dma, dma((NX, 4)), dma, dma,
        ],
        compiler_params=pltpu.CompilerParams(
            collective_id=0, has_side_effects=True, vmem_limit_bytes=40 << 20
        ),
    )(
        *(pltpu.with_memory_space_constraint(v, pltpu.HBM) for v in (
            tile_rows.reshape(1, TILES), tile_cols.reshape(1, TILES), row_counts, bounds, orbitals_t, tiles, rotation,
        ))
    )


def solution(mesh):
    return jax.shard_map(
        local,
        mesh=mesh,
        in_specs=(
            P("orb", "slab"),
            P("slab", None, None),
            P("slab"),
            P("slab"),
            P("slab"),
            P(),
            P("orb", None),
        ),
        out_specs=P("orb", "slab"),
        check_vma=False,
    )
```
